32 devices in a mesh: dp: 8 (over z, x), tensor: 4 (over y, core).
Axes of the slice: x: 2, y: 2, z: 4, core: 2. Of those that a mesh axis runs over, the one named last changes fastest.
Arguments:
- hidden_in: bfloat16 [16384, 2560], P('dp'), may hold values from -6 to 6
- segment_ids: int32 [8, 2048], P('dp'), may hold values from 0 to 3, as said below
- positions: int32 [8, 2048], P('dp'), may hold values from 0 to 4095, as said below
- cotangent: bfloat16 [16384, 2560], P('dp'), may hold values from -6 to 6
- query_weight: bfloat16 [2560, 2048], P('dp', 'tensor'), may hold values from -0.125 to 0.125
- key_projection: bfloat16 [2560, 1024], P('dp', 'tensor'), may hold values from -0.125 to 0.125
- value_projection: bfloat16 [2560, 1024], P('dp', 'tensor'), may hold values from -0.125 to 0.125
- output_weight: bfloat16 [2048, 2560], P('tensor', 'dp'), may hold values from -0.125 to 0.125
- gate_weight: bfloat16 [2560, 10240], P('dp', 'tensor'), may hold values from -0.125 to 0.125
- upward_weight: bfloat16 [2560, 10240], P('dp', 'tensor'), may hold values from -0.125 to 0.125
- down_weight: bfloat16 [10240, 2560], P('tensor', 'dp'), may hold values from -0.0625 to 0.0625
- norm_gains: bfloat16 [4, 2560], P(None, 'dp'), may hold values from -0.8984375 to 0.8984375
- head_gains: bfloat16 [2, 256], P(None, 'dp'), may hold values from -0.8984375 to 0.8984375
- query_mean: float32 [2560, 2048], P('dp', 'tensor'), may hold values from -6 to 6
- query_square: float32 [2560, 2048], P('dp', 'tensor'), may hold values from 1 to 100
- key_first_moment: float32 [2560, 1024], P('dp', 'tensor'), may hold values from -6 to 6
- key_second_moment: float32 [2560, 1024], P('dp', 'tensor'), may hold values from 1 to 100
- value_first_moment: float32 [2560, 1024], P('dp', 'tensor'), may hold values from -6 to 6
- value_second_moment: float32 [2560, 1024], P('dp', 'tensor'), may hold values from 1 to 100
- output_mean: float32 [2048, 2560], P('tensor', 'dp'), may hold values from -6 to 6
- output_square: float32 [2048, 2560], P('tensor', 'dp'), may hold values from 1 to 100
- gate_mean: float32 [2560, 10240], P('dp', 'tensor'), may hold values from -6 to 6
- gate_square: float32 [2560, 10240], P('dp', 'tensor'), may hold values from 1 to 100
- upward_mean: float32 [2560, 10240], P('dp', 'tensor'), may hold values from -6 to 6
- upward_square: float32 [2560, 10240], P('dp', 'tensor'), may hold values from 1 to 100
- down_mean: float32 [10240, 2560], P('tensor', 'dp'), may hold values from -6 to 6
- down_square: float32 [10240, 2560], P('tensor', 'dp'), may hold values from 1 to 100
- norms_mean: float32 [4, 2560], P(None, 'dp'), may hold values from -6 to 6
- norms_square: float32 [4, 2560], P(None, 'dp'), may hold values from 1 to 100
- heads_mean: float32 [2, 256], P(None, 'dp'), may hold values from -6 to 6
- heads_square: float32 [2, 256], P(None, 'dp'), may hold values from 1 to 100
Outputs:
- block_output: bfloat16 [16384, 2560], P('dp')
- input_gradient: float32 [16384, 2560], P('dp')
- query_gradient: float32 [2560, 2048], P('dp', 'tensor')
- key_gradient: float32 [2560, 1024], P('dp', 'tensor')
- value_gradient: float32 [2560, 1024], P('dp', 'tensor')
- output_gradient: float32 [2048, 2560], P('tensor', 'dp')
- gate_gradient: float32 [2560, 10240], P('dp', 'tensor')
- upward_gradient: float32 [2560, 10240], P('dp', 'tensor')
- down_gradient: float32 [10240, 2560], P('tensor', 'dp')
- norms_gradient: float32 [4, 2560], P(None, 'dp')
- heads_gradient: float32 [2, 256], P(None, 'dp')
- query_updated: float32 [2560, 2048], P('dp', 'tensor')
- key_updated: float32 [2560, 1024], P('dp', 'tensor')
- value_updated: float32 [2560, 1024], P('dp', 'tensor')
- output_updated: float32 [2048, 2560], P('tensor', 'dp')
- gate_updated: float32 [2560, 10240], P('dp', 'tensor')
- upward_updated: float32 [2560, 10240], P('dp', 'tensor')
- down_updated: float32 [10240, 2560], P('tensor', 'dp')
- norms_updated: float32 [4, 2560], P(None, 'dp')
- heads_updated: float32 [2, 256], P(None, 'dp')
- query_newmean: float32 [2560, 2048], P('dp', 'tensor')
- key_newmean: float32 [2560, 1024], P('dp', 'tensor')
- value_newmean: float32 [2560, 1024], P('dp', 'tensor')
- output_newmean: float32 [2048, 2560], P('tensor', 'dp')
- gate_newmean: float32 [2560, 10240], P('dp', 'tensor')
- upward_newmean: float32 [2560, 10240], P('dp', 'tensor')
- down_newmean: float32 [10240, 2560], P('tensor', 'dp')
- norms_newmean: float32 [4, 2560], P(None, 'dp')
- heads_newmean: float32 [2, 256], P(None, 'dp')
- query_newsquare: float32 [2560, 2048], P('dp', 'tensor')
- key_newsquare: float32 [2560, 1024], P('dp', 'tensor')
- value_newsquare: float32 [2560, 1024], P('dp', 'tensor')
- output_newsquare: float32 [2048, 2560], P('tensor', 'dp')
- gate_newsquare: float32 [2560, 10240], P('dp', 'tensor')
- upward_newsquare: float32 [2560, 10240], P('dp', 'tensor')
- down_newsquare: float32 [10240, 2560], P('tensor', 'dp')
- norms_newsquare: float32 [4, 2560], P(None, 'dp')
- heads_newsquare: float32 [2, 256], P(None, 'dp')
The draws below stay inside these ranges and needn't reach their ends.
Inputs may be any that keep to these rules, and one draw needn't show every extreme that they name: `segment_ids`: in each row, ids never fall and every id of 0 to 3 names one or more tokens. Within a document, positions rise by one from token to token; each row's first document starts at 0.
All inputs are finite; a program needn't handle non-finite values.
Results may differ from the reference program's by a relative error of at most 0.038.
Values may be sent and summed in bfloat16 or wider, within the bound.
No kernel may reach another device: no remote copies, remote signals or barrier semaphores. Data moves between devices by JAX's collectives and lax.ppermute only.
A program may use at most 448 MiB of HBM per device.

```python
import math
import jax
import jax.numpy as jnp
from jax import lax

MODEL_WIDTH = 2560
HQ = 8
KEY_VALUE_HEADS = 4
HEAD_WIDTH = 256
FF = 10240
WINDOW = 1024
SEQ = 2048
DOCS = 4
STEP = 4
SEQS = 8
TOKENS = 16384
N_DP = 8
N_TENSOR = 4


def document_layout(key):
    cut_keys = jax.random.split(jax.random.fold_in(key, 7), SEQS)

    def row_cuts(row_key):
        return jnp.sort(jax.random.permutation(row_key, SEQ - 1)[:DOCS - 1] + 1).astype(jnp.int32)
    cuts = jax.vmap(row_cuts)(cut_keys)
    index = jnp.arange(SEQ, dtype=jnp.int32)
    segments = jnp.sum((index[None, :, None] >= cuts[:, None, :]).astype(jnp.int32), axis=-1)
    doc_starts = jnp.concatenate([jnp.zeros((SEQS, 1), jnp.int32), cuts], axis=1)
    return (segments.astype(jnp.int32), doc_starts)


def draw_segment_ids(key, part):
    segments, doc_starts = document_layout(key)
    return segments


def draw_positions(key, part):
    segments, doc_starts = document_layout(key)
    offsets = jax.random.randint(jax.random.fold_in(key, 11), (SEQS, DOCS), 0, SEQ).astype(jnp.int32)
    doc_index = jnp.arange(DOCS, dtype=jnp.int32)[None, :]
    last_offset = SEQ + doc_starts[:, DOCS - 1:DOCS]
    offsets = jnp.where(doc_index == 0, 0, offsets)
    offsets = jnp.where(doc_index == DOCS - 1, last_offset, offsets).astype(jnp.int32)
    chosen = segments[:, :, None] == jnp.arange(DOCS, dtype=jnp.int32)[None, None, :]
    start_of = jnp.sum(jnp.where(chosen, doc_starts[:, None, :], 0), axis=-1)
    offset_of = jnp.sum(jnp.where(chosen, offsets[:, None, :], 0), axis=-1)
    index = jnp.arange(SEQ, dtype=jnp.int32)
    return (index[None, :] - start_of + offset_of).astype(jnp.int32)


def block_scale(rng, extent, cuts, least, high):
    factor_of = 1.0
    for axis_at, shards_of in cuts:
        steps = jax.random.uniform(jax.random.fold_in(jax.random.fold_in(rng, 6), axis_at), (shards_of,), jnp.float32, least / len(cuts), high / len(cuts))
        factor_of = factor_of * jnp.repeat(jnp.exp(steps), extent[axis_at] // shards_of).reshape((-1,) + (1,) * (len(extent) - 1 - axis_at))
    return factor_of


def bell_draw(rng, dims, width, limit, shards=(), kind=jnp.bfloat16):
    entries = width * jax.random.normal(rng, dims, jnp.float32)
    if shards:
        entries = entries * block_scale(rng, dims, shards, -0.22, 0.18)
    return jnp.clip(entries, -limit, limit).astype(kind)


def setup_inputs(seed: int = 0) -> dict:
    key_list = jax.random.split(jax.random.key(seed), 32)
    hidden_in = bell_draw(key_list[0], (TOKENS, MODEL_WIDTH), 1.0, 6.0, ((0, 8),))
    segment_ids = draw_segment_ids(jax.random.fold_in(key_list[31], 71), 0)
    positions = draw_positions(jax.random.fold_in(key_list[31], 71), 0)
    cotangent = bell_draw(key_list[3], (TOKENS, MODEL_WIDTH), 1.0, 6.0, ((0, 8),))
    query_weight = bell_draw(key_list[4], (MODEL_WIDTH, HQ * HEAD_WIDTH), MODEL_WIDTH ** -0.5, 0.125, ((0, 8), (1, 4)))
    key_projection = bell_draw(key_list[5], (MODEL_WIDTH, KEY_VALUE_HEADS * HEAD_WIDTH), MODEL_WIDTH ** -0.5, 0.125, ((0, 8), (1, 4)))
    value_projection = bell_draw(key_list[6], (MODEL_WIDTH, KEY_VALUE_HEADS * HEAD_WIDTH), MODEL_WIDTH ** -0.5, 0.125, ((0, 8), (1, 4)))
    output_weight = bell_draw(key_list[7], (HQ * HEAD_WIDTH, MODEL_WIDTH), (HQ * HEAD_WIDTH) ** -0.5, 0.125, ((0, 4), (1, 8)))
    gate_weight = bell_draw(key_list[8], (MODEL_WIDTH, FF), MODEL_WIDTH ** -0.5, 0.125, ((0, 8), (1, 4)))
    upward_weight = bell_draw(key_list[9], (MODEL_WIDTH, FF), MODEL_WIDTH ** -0.5, 0.125, ((0, 8), (1, 4)))
    down_weight = bell_draw(key_list[10], (FF, MODEL_WIDTH), FF ** -0.5, 0.0625, ((0, 4), (1, 8)))
    norm_gains = bell_draw(key_list[11], (4, MODEL_WIDTH), 0.3, 0.8984375, ((1, 8),))
    head_gains = bell_draw(key_list[12], (2, HEAD_WIDTH), 0.3, 0.8984375, ((1, 8),))
    query_mean = bell_draw(key_list[13], (MODEL_WIDTH, HQ * HEAD_WIDTH), 1.0, 6.0, ((0, 8), (1, 4)), jnp.float32)
    query_square = jnp.clip(jnp.exp(math.log(100.0) - 4.6051702 * jax.random.uniform(key_list[14], (MODEL_WIDTH, HQ * HEAD_WIDTH), jnp.float32) ** block_scale(key_list[14], (MODEL_WIDTH, HQ * HEAD_WIDTH), ((0, 8), (1, 4)), -0.2, 0.2)), 1.0, 100.0)
    key_first_moment = bell_draw(key_list[15], (MODEL_WIDTH, KEY_VALUE_HEADS * HEAD_WIDTH), 1.0, 6.0, ((0, 8), (1, 4)), jnp.float32)
    key_second_moment = jnp.clip(jnp.exp(math.log(100.0) - 4.6051702 * jax.random.uniform(key_list[16], (MODEL_WIDTH, KEY_VALUE_HEADS * HEAD_WIDTH), jnp.float32) ** block_scale(key_list[16], (MODEL_WIDTH, KEY_VALUE_HEADS * HEAD_WIDTH), ((0, 8), (1, 4)), -0.2, 0.2)), 1.0, 100.0)
    value_first_moment = bell_draw(key_list[17], (MODEL_WIDTH, KEY_VALUE_HEADS * HEAD_WIDTH), 1.0, 6.0, ((0, 8), (1, 4)), jnp.float32)
    value_second_moment = jnp.clip(jnp.exp(math.log(100.0) - 4.6051702 * jax.random.uniform(key_list[18], (MODEL_WIDTH, KEY_VALUE_HEADS * HEAD_WIDTH), jnp.float32) ** block_scale(key_list[18], (MODEL_WIDTH, KEY_VALUE_HEADS * HEAD_WIDTH), ((0, 8), (1, 4)), -0.2, 0.2)), 1.0, 100.0)
    output_mean = bell_draw(key_list[19], (HQ * HEAD_WIDTH, MODEL_WIDTH), 1.0, 6.0, ((0, 4), (1, 8)), jnp.float32)
    output_square = jnp.clip(jnp.exp(math.log(100.0) - 4.6051702 * jax.random.uniform(key_list[20], (HQ * HEAD_WIDTH, MODEL_WIDTH), jnp.float32) ** block_scale(key_list[20], (HQ * HEAD_WIDTH, MODEL_WIDTH), ((0, 4), (1, 8)), -0.2, 0.2)), 1.0, 100.0)
    gate_mean = bell_draw(key_list[21], (MODEL_WIDTH, FF), 1.0, 6.0, ((0, 8), (1, 4)), jnp.float32)
    gate_square = jnp.clip(jnp.exp(math.log(100.0) - 4.6051702 * jax.random.uniform(key_list[22], (MODEL_WIDTH, FF), jnp.float32) ** block_scale(key_list[22], (MODEL_WIDTH, FF), ((0, 8), (1, 4)), -0.2, 0.2)), 1.0, 100.0)
    upward_mean = bell_draw(key_list[23], (MODEL_WIDTH, FF), 1.0, 6.0, ((0, 8), (1, 4)), jnp.float32)
    upward_square = jnp.clip(jnp.exp(math.log(100.0) - 4.6051702 * jax.random.uniform(key_list[24], (MODEL_WIDTH, FF), jnp.float32) ** block_scale(key_list[24], (MODEL_WIDTH, FF), ((0, 8), (1, 4)), -0.2, 0.2)), 1.0, 100.0)
    down_mean = bell_draw(key_list[25], (FF, MODEL_WIDTH), 1.0, 6.0, ((0, 4), (1, 8)), jnp.float32)
    down_square = jnp.clip(jnp.exp(math.log(100.0) - 4.6051702 * jax.random.uniform(key_list[26], (FF, MODEL_WIDTH), jnp.float32) ** block_scale(key_list[26], (FF, MODEL_WIDTH), ((0, 4), (1, 8)), -0.2, 0.2)), 1.0, 100.0)
    norms_mean = bell_draw(key_list[27], (4, MODEL_WIDTH), 1.0, 6.0, ((1, 8),), jnp.float32)
    norms_square = jnp.clip(jnp.exp(math.log(100.0) - 4.6051702 * jax.random.uniform(key_list[28], (4, MODEL_WIDTH), jnp.float32) ** block_scale(key_list[28], (4, MODEL_WIDTH), ((1, 8),), -0.2, 0.2)), 1.0, 100.0)
    heads_mean = bell_draw(key_list[29], (2, HEAD_WIDTH), 1.0, 6.0, ((1, 8),), jnp.float32)
    heads_square = jnp.clip(jnp.exp(math.log(100.0) - 4.6051702 * jax.random.uniform(key_list[30], (2, HEAD_WIDTH), jnp.float32) ** block_scale(key_list[30], (2, HEAD_WIDTH), ((1, 8),), -0.2, 0.2)), 1.0, 100.0)
    return dict(hidden_in=hidden_in, segment_ids=segment_ids, positions=positions, cotangent=cotangent, query_weight=query_weight, key_projection=key_projection, value_projection=value_projection, output_weight=output_weight, gate_weight=gate_weight, upward_weight=upward_weight, down_weight=down_weight, norm_gains=norm_gains, head_gains=head_gains, query_mean=query_mean, query_square=query_square, key_first_moment=key_first_moment, key_second_moment=key_second_moment, value_first_moment=value_first_moment, value_second_moment=value_second_moment, output_mean=output_mean, output_square=output_square, gate_mean=gate_mean, gate_square=gate_square, upward_mean=upward_mean, upward_square=upward_square, down_mean=down_mean, down_square=down_square, norms_mean=norms_mean, norms_square=norms_square, heads_mean=heads_mean, heads_square=heads_square)


NORM_EPS = 1e-06
BETA_ONE = 0.9
BETA_TWO = 0.999
ADAM_EPS = 1e-08
LEARN_RATE = 0.01
DECAY_RATE = 0.1
ROPE_BASE = 10000.0
GELU_COEF = 0.7978845608028654
MASKED = -1e+30

def mixing(form, left_side, right_side):
    return jnp.einsum(form, left_side.astype(jnp.float32), right_side.astype(jnp.float32))

def rms_forward(values, gain_row):
    factor = lax.rsqrt(lax.optimization_barrier(jnp.mean(values * values, axis=-1, keepdims=True)) + NORM_EPS)
    normed = values * factor
    return (normed * (1.0 + gain_row), normed, factor)

def rms_backward(upstream, normed, factor, gain_row):
    scaled = upstream * (1.0 + gain_row)
    return factor * (scaled - normed * lax.optimization_barrier(jnp.mean(scaled * normed, axis=-1, keepdims=True)))

def rope_tables(places, head_size):
    half_dim = head_size // 2
    frequency = ROPE_BASE ** (-2.0 * jnp.arange(half_dim, dtype=jnp.float32) / head_size)
    angles = places.astype(jnp.float32)[:, None] * frequency[None, :]
    return (jnp.cos(angles)[:, None, :], jnp.sin(angles)[:, None, :])

def rotate(values, cosine, sine_table):
    half_dim = values.shape[-1] // 2
    first_half = values[..., :half_dim]
    second_half = values[..., half_dim:]
    return jnp.concatenate([first_half * cosine - second_half * sine_table, second_half * cosine + first_half * sine_table], axis=-1)

def rotate_back(values, cosine, sine_table):
    half_dim = values.shape[-1] // 2
    first_half = values[..., :half_dim]
    second_half = values[..., half_dim:]
    return jnp.concatenate([first_half * cosine + second_half * sine_table, second_half * cosine - first_half * sine_table], axis=-1)

def gelu_value(values):
    inner = GELU_COEF * (values + 0.044715 * values ** 3)
    return 0.5 * values * (1.0 + jnp.tanh(inner))

def gelu_slope(values):
    tangent = jnp.tanh(GELU_COEF * (values + 0.044715 * values ** 3))
    return 0.5 * (1.0 + tangent) + 0.5 * values * (1.0 - tangent * tangent) * GELU_COEF * (1.0 + 3.0 * 0.044715 * values * values)

def layout(length):
    block_rows = min(512, length)
    key_span = (WINDOW + block_rows - 1) // block_rows * block_rows
    return (block_rows, key_span)

def window_mask(segments, seg_padded, offset, block_rows, key_span):
    query_index = offset + jnp.arange(block_rows, dtype=jnp.int32)
    key_index = offset - key_span + jnp.arange(key_span + block_rows, dtype=jnp.int32)
    query_seg = lax.dynamic_slice_in_dim(segments, offset, block_rows, 0)
    key_seg = lax.dynamic_slice_in_dim(seg_padded, offset, key_span + block_rows, 0)
    causal = (key_index[None, :] <= query_index[:, None]) & (key_index[None, :] > query_index[:, None] - WINDOW)
    return causal & (query_seg[:, None] == key_seg[None, :])

def attend_forward(query_heads, key_heads, value_heads, segments):
    length = query_heads.shape[0]
    block_rows, key_span = layout(length)
    score_scale = query_heads.shape[-1] ** (-0.5)
    key_pad = jnp.pad(key_heads, ((key_span, 0), (0, 0), (0, 0)))
    value_pad = jnp.pad(value_heads, ((key_span, 0), (0, 0), (0, 0)))
    seg_padded = jnp.concatenate([jnp.full((key_span,), -1, jnp.int32), segments.astype(jnp.int32)])

    def step_block(state_carry, offset):
        query_block = lax.dynamic_slice_in_dim(query_heads, offset, block_rows, 0)
        key_block = lax.dynamic_slice_in_dim(key_pad, offset, key_span + block_rows, 0)
        value_block = lax.dynamic_slice_in_dim(value_pad, offset, key_span + block_rows, 0)
        allowed = window_mask(segments, seg_padded, offset, block_rows, key_span)
        scores = mixing('qgrd,kgd->grqk', query_block, key_block) * score_scale
        scores = jnp.where(allowed[None, None], scores, MASKED)
        top_score = lax.optimization_barrier(jnp.max(scores, axis=-1, keepdims=True))
        raw_weights = jnp.exp(scores - top_score)
        denominator = lax.optimization_barrier(jnp.sum(raw_weights, axis=-1, keepdims=True))
        probability = (raw_weights / denominator).astype(jnp.bfloat16)
        result = mixing('grqk,kgd->qgrd', probability, value_block).astype(jnp.bfloat16)
        return (state_carry, (result, (top_score + jnp.log(denominator))[..., 0]))
    starts = jnp.arange(length // block_rows, dtype=jnp.int32) * block_rows
    unused, (blocks, lse_blocks) = lax.scan(step_block, jnp.int32(0), starts)
    return (blocks.reshape(query_heads.shape), lse_blocks)

def attend_backward(query_heads, key_heads, value_heads, segments, attended, lse_blocks, upstream):
    length = query_heads.shape[0]
    block_rows, key_span = layout(length)
    score_scale = query_heads.shape[-1] ** (-0.5)
    key_pad = jnp.pad(key_heads, ((key_span, 0), (0, 0), (0, 0)))
    value_pad = jnp.pad(value_heads, ((key_span, 0), (0, 0), (0, 0)))
    seg_padded = jnp.concatenate([jnp.full((key_span,), -1, jnp.int32), segments.astype(jnp.int32)])
    delta = lax.optimization_barrier(jnp.sum(upstream * attended.astype(jnp.float32), axis=-1))
    upstream_half = upstream.astype(jnp.bfloat16)
    zero_acc = jnp.zeros((key_span + length,) + key_heads.shape[1:], jnp.float32)

    def step_block(state_carry, inputs):
        offset, lse_block = inputs
        key_acc, value_acc = state_carry
        query_block = lax.dynamic_slice_in_dim(query_heads, offset, block_rows, 0)
        key_block = lax.dynamic_slice_in_dim(key_pad, offset, key_span + block_rows, 0)
        value_block = lax.dynamic_slice_in_dim(value_pad, offset, key_span + block_rows, 0)
        grad_block = lax.dynamic_slice_in_dim(upstream_half, offset, block_rows, 0)
        delta_block = jnp.transpose(lax.dynamic_slice_in_dim(delta, offset, block_rows, 0), (1, 2, 0))
        allowed = window_mask(segments, seg_padded, offset, block_rows, key_span)
        scores = mixing('qgrd,kgd->grqk', query_block, key_block) * score_scale
        scores = jnp.where(allowed[None, None], scores, MASKED)
        probability = jnp.exp(scores - lse_block[..., None])
        prob_half = probability.astype(jnp.bfloat16)
        value_grad = mixing('grqk,qgrd->kgd', prob_half, grad_block)
        prob_grad = mixing('qgrd,kgd->grqk', grad_block, value_block)
        score_grad = (probability * (prob_grad - delta_block[..., None])).astype(jnp.bfloat16)
        query_grad = mixing('grqk,kgd->qgrd', score_grad, key_block) * score_scale
        key_grad = mixing('grqk,qgrd->kgd', score_grad, query_block) * score_scale
        key_acc = lax.dynamic_update_slice_in_dim(key_acc, lax.dynamic_slice_in_dim(key_acc, offset, key_span + block_rows, 0) + key_grad, offset, 0)
        value_acc = lax.dynamic_update_slice_in_dim(value_acc, lax.dynamic_slice_in_dim(value_acc, offset, key_span + block_rows, 0) + value_grad, offset, 0)
        return ((key_acc, value_acc), query_grad)
    starts = jnp.arange(length // block_rows, dtype=jnp.int32) * block_rows
    (key_acc, value_acc), query_grads = lax.scan(step_block, (zero_acc, zero_acc), (starts, lse_blocks))
    return (query_grads.reshape(query_heads.shape), key_acc[key_span:], value_acc[key_span:])

def front_forward(normed_rows, query_full, key_full, value_full, head_gain, cosine, sine_table, head_size):
    rows_count = normed_rows.shape[0]
    query_raw = jnp.dot(normed_rows, query_full, preferred_element_type=jnp.float32).reshape(rows_count, -1, head_size)
    key_raw = jnp.dot(normed_rows, key_full, preferred_element_type=jnp.float32).reshape(rows_count, -1, head_size)
    value_heads = jnp.dot(normed_rows, value_full, preferred_element_type=jnp.float32).astype(jnp.bfloat16).reshape(rows_count, -1, head_size)
    query_normed, query_unit, query_factor = rms_forward(query_raw, head_gain[0])
    key_normed, key_unit, key_factor = rms_forward(key_raw, head_gain[1])
    query_heads = rotate(query_normed, cosine, sine_table).astype(jnp.bfloat16)
    key_heads = rotate(key_normed, cosine, sine_table).astype(jnp.bfloat16)
    query_heads = query_heads.reshape(rows_count, key_heads.shape[1], -1, head_size)
    return (query_heads, key_heads, value_heads, (query_unit, query_factor, key_unit, key_factor))

def front_backward(normed_rows, query_full, key_full, value_full, head_gain, cosine, sine_table, saved, query_grad, key_grad, value_grad):
    query_unit, query_factor, key_unit, key_factor = saved
    rows_count = normed_rows.shape[0]
    query_rot = rotate_back(query_grad.reshape(query_unit.shape), cosine, sine_table)
    key_rot = rotate_back(key_grad, cosine, sine_table)
    gain_grads = jnp.stack([lax.optimization_barrier(jnp.sum(query_rot * query_unit, axis=(0, 1))), lax.optimization_barrier(jnp.sum(key_rot * key_unit, axis=(0, 1)))])
    query_flat = rms_backward(query_rot, query_unit, query_factor, head_gain[0]).astype(jnp.bfloat16).reshape(rows_count, -1)
    key_flat = rms_backward(key_rot, key_unit, key_factor, head_gain[1]).astype(jnp.bfloat16).reshape(rows_count, -1)
    value_flat = value_grad.astype(jnp.bfloat16).reshape(rows_count, -1)
    input_part = jnp.dot(query_flat, query_full.T, preferred_element_type=jnp.float32)
    input_part = input_part + jnp.dot(key_flat, key_full.T, preferred_element_type=jnp.float32)
    input_part = input_part + jnp.dot(value_flat, value_full.T, preferred_element_type=jnp.float32)
    weight_grads = (jnp.dot(normed_rows.T, query_flat, preferred_element_type=jnp.float32), jnp.dot(normed_rows.T, key_flat, preferred_element_type=jnp.float32), jnp.dot(normed_rows.T, value_flat, preferred_element_type=jnp.float32))
    return (input_part, gain_grads, weight_grads)

def feed_forward(normed_rows, gate_full, upward_full, down_full):
    gate_pre = jnp.dot(normed_rows, gate_full, preferred_element_type=jnp.float32)
    upward_pre = jnp.dot(normed_rows, upward_full, preferred_element_type=jnp.float32)
    mixed = (gelu_value(gate_pre) * upward_pre).astype(jnp.bfloat16)
    return (jnp.dot(mixed, down_full, preferred_element_type=jnp.float32), (gate_pre, upward_pre, mixed))

def feed_backward(normed_rows, gate_full, upward_full, down_full, saved, upstream_half):
    gate_pre, upward_pre, mixed = saved
    hidden_grad = jnp.dot(upstream_half, down_full.T, preferred_element_type=jnp.float32)
    gate_back = (hidden_grad * upward_pre * gelu_slope(gate_pre)).astype(jnp.bfloat16)
    upward_back = (hidden_grad * gelu_value(gate_pre)).astype(jnp.bfloat16)
    input_part = jnp.dot(gate_back, gate_full.T, preferred_element_type=jnp.float32)
    input_part = input_part + jnp.dot(upward_back, upward_full.T, preferred_element_type=jnp.float32)
    weight_grads = (jnp.dot(normed_rows.T, gate_back, preferred_element_type=jnp.float32), jnp.dot(normed_rows.T, upward_back, preferred_element_type=jnp.float32), jnp.dot(mixed.T, upstream_half, preferred_element_type=jnp.float32))
    return (input_part, weight_grads)

def adam_update(weight_shard, grad_shard, mean_shard, square_shard, decay):
    new_mean = BETA_ONE * mean_shard + (1.0 - BETA_ONE) * grad_shard
    new_square = BETA_TWO * square_shard + (1.0 - BETA_TWO) * grad_shard * grad_shard
    mean_hat = new_mean / (1.0 - BETA_ONE ** STEP)
    square_hat = new_square / (1.0 - BETA_TWO ** STEP)
    weight_value = weight_shard.astype(jnp.float32)
    updated = weight_value - LEARN_RATE * (mean_hat / (jnp.sqrt(square_hat) + ADAM_EPS) + decay * weight_value)
    return (updated, new_mean, new_square)

def tensor_total(parts):
    accumulated = jnp.zeros_like(parts[0])
    for piece in parts:
        accumulated = accumulated + lax.optimization_barrier(piece.astype(jnp.bfloat16)).astype(jnp.float32)
    return accumulated

def reference(hidden_in, segment_ids, positions, cotangent, query_weight, key_projection, value_projection, output_weight, gate_weight, upward_weight, down_weight, norm_gains, head_gains, query_mean, query_square, key_first_moment, key_second_moment, value_first_moment, value_second_moment, output_mean, output_square, gate_mean, gate_square, upward_mean, upward_square, down_mean, down_square, norms_mean, norms_square, heads_mean, heads_square):
    query_groups = N_TENSOR
    query_cols = HQ * HEAD_WIDTH // query_groups
    key_columns = KEY_VALUE_HEADS * HEAD_WIDTH // query_groups
    hidden_cols = FF // query_groups

    def split_groups(matrix, part_width, along):
        return [lax.slice_in_dim(matrix, member * part_width, (member + 1) * part_width, axis=along) for member in range(query_groups)]
    query_parts = split_groups(query_weight, query_cols, 1)
    key_parts = split_groups(key_projection, key_columns, 1)
    value_parts = split_groups(value_projection, key_columns, 1)
    output_parts = split_groups(output_weight, query_cols, 0)
    gate_parts = split_groups(gate_weight, hidden_cols, 1)
    upward_parts = split_groups(upward_weight, hidden_cols, 1)
    down_parts = split_groups(down_weight, hidden_cols, 0)
    norm_gain = norm_gains.astype(jnp.float32)
    head_gain = head_gains.astype(jnp.float32)

    def sequence_pass(totals, inputs):
        rows_half, segments, places, upstream_half = inputs
        rows_count = rows_half.shape[0]
        rows_in = rows_half.astype(jnp.float32)
        cosine, sine_table = rope_tables(places, HEAD_WIDTH)
        attn_in, unit_one, factor_one = rms_forward(rows_in, norm_gain[0])
        attn_in = attn_in.astype(jnp.bfloat16)
        fronts = [front_forward(attn_in, query_parts[member], key_parts[member], value_parts[member], head_gain, cosine, sine_table, HEAD_WIDTH) for member in range(query_groups)]
        attends = [attend_forward(front[0], front[1], front[2], segments) for front in fronts]
        attn_sum = tensor_total([jnp.dot(attends[member][0].reshape(rows_count, -1), output_parts[member], preferred_element_type=jnp.float32) for member in range(query_groups)])
        attn_out, unit_two, factor_two = rms_forward(attn_sum, norm_gain[1])
        middle = rows_in + attn_out
        ffn_in, unit_three, factor_three = rms_forward(middle, norm_gain[2])
        ffn_in = ffn_in.astype(jnp.bfloat16)
        ffns = [feed_forward(ffn_in, gate_parts[member], upward_parts[member], down_parts[member]) for member in range(query_groups)]
        ffn_sum = tensor_total([item[0] for item in ffns])
        ffn_out, unit_four, factor_four = rms_forward(ffn_sum, norm_gain[3])
        block_output = (middle + ffn_out).astype(jnp.bfloat16)
        upstream = upstream_half.astype(jnp.float32)
        gain_four = lax.optimization_barrier(jnp.sum(upstream * unit_four, axis=0))
        ffn_grad = rms_backward(upstream, unit_four, factor_four, norm_gain[3]).astype(jnp.bfloat16)
        ffn_backs = [feed_backward(ffn_in, gate_parts[member], upward_parts[member], down_parts[member], ffns[member][1], ffn_grad) for member in range(query_groups)]
        ffn_in_grad = tensor_total([item[0] for item in ffn_backs])
        gain_three = lax.optimization_barrier(jnp.sum(ffn_in_grad * unit_three, axis=0))
        middle_grad = upstream + rms_backward(ffn_in_grad, unit_three, factor_three, norm_gain[2])
        gain_two = lax.optimization_barrier(jnp.sum(middle_grad * unit_two, axis=0))
        attn_grad = rms_backward(middle_grad, unit_two, factor_two, norm_gain[1]).astype(jnp.bfloat16)
        output_grads = []
        front_backs = []
        for member in range(query_groups):
            attended = attends[member][0]
            attended_flat = attended.reshape(rows_count, -1)
            output_grads.append(jnp.dot(attended_flat.T, attn_grad, preferred_element_type=jnp.float32))
            attended_grad = jnp.dot(attn_grad, output_parts[member].T, preferred_element_type=jnp.float32).reshape(attended.shape)
            front = fronts[member]
            query_grad, key_grad, value_grad = attend_backward(front[0], front[1], front[2], segments, attended, attends[member][1], attended_grad)
            front_backs.append(front_backward(attn_in, query_parts[member], key_parts[member], value_parts[member], head_gain, cosine, sine_table, front[3], query_grad, key_grad, value_grad))
        attn_in_grad = tensor_total([item[0] for item in front_backs])
        head_grad = tensor_total([item[1] for item in front_backs])
        gain_one = lax.optimization_barrier(jnp.sum(attn_in_grad * unit_one, axis=0))
        input_grad = middle_grad + rms_backward(attn_in_grad, unit_one, factor_one, norm_gain[0])
        additions = (jnp.concatenate([item[2][0] for item in front_backs], axis=1), jnp.concatenate([item[2][1] for item in front_backs], axis=1), jnp.concatenate([item[2][2] for item in front_backs], axis=1), jnp.concatenate(output_grads, axis=0), jnp.concatenate([item[1][0] for item in ffn_backs], axis=1), jnp.concatenate([item[1][1] for item in ffn_backs], axis=1), jnp.concatenate([item[1][2] for item in ffn_backs], axis=0), jnp.stack([gain_one, gain_two, gain_three, gain_four]), head_grad)
        totals = tuple((total_item + added for total_item, added in zip(totals, additions)))
        return (totals, (block_output, input_grad))
    params = (query_weight, key_projection, value_projection, output_weight, gate_weight, upward_weight, down_weight, norm_gains, head_gains)
    zero_totals = tuple((jnp.zeros(param.shape, jnp.float32) for param in params))
    inputs = (hidden_in.reshape(N_DP, SEQ, MODEL_WIDTH), segment_ids, positions, cotangent.reshape(N_DP, SEQ, MODEL_WIDTH))
    grads, (outputs, input_grads) = lax.scan(sequence_pass, zero_totals, inputs)
    means = (query_mean, key_first_moment, value_first_moment, output_mean, gate_mean, upward_mean, down_mean, norms_mean, heads_mean)
    squares = (query_square, key_second_moment, value_second_moment, output_square, gate_square, upward_square, down_square, norms_square, heads_square)
    decays = (DECAY_RATE,) * 7 + (0.0, 0.0)
    results = [adam_update(param, grad_item, mean_item, square_item, decay) for param, grad_item, mean_item, square_item, decay in zip(params, grads, means, squares, decays)]
    return (outputs.reshape(TOKENS, MODEL_WIDTH), input_grads.reshape(TOKENS, MODEL_WIDTH), grads[0], grads[1], grads[2], grads[3], grads[4], grads[5], grads[6], grads[7], grads[8], results[0][0], results[1][0], results[2][0], results[3][0], results[4][0], results[5][0], results[6][0], results[7][0], results[8][0], results[0][1], results[1][1], results[2][1], results[3][1], results[4][1], results[5][1], results[6][1], results[7][1], results[8][1], results[0][2], results[1][2], results[2][2], results[3][2], results[4][2], results[5][2], results[6][2], results[7][2], results[8][2])
```

```python
import functools

import jax
import jax.numpy as jnp
from jax import lax
from jax.experimental import pallas as pl
from jax.experimental.pallas import tpu as pltpu
from jax.sharding import PartitionSpec as P

HEAD_WIDTH = 256
WINDOW = 1024
STEP = 4
CHUNKS = 2
BLOCK = 256

NORM_EPS = 1e-06
BETA_ONE = 0.9
BETA_TWO = 0.999
ADAM_EPS = 1e-08
LEARN_RATE = 0.01
DECAY_RATE = 0.1
ROPE_BASE = 10000.0
GELU_COEF = 0.7978845608028654
MASKED = -1e30


F32 = jnp.float32
HALF = jnp.bfloat16


def mm(a, b):
    return lax.dot_general(a, b, (((1,), (0,)), ((), ())), preferred_element_type=F32)


def mm_nt(a, b):
    return lax.dot_general(a, b, (((1,), (1,)), ((), ())), preferred_element_type=F32)


def mm_tn(a, b):
    return lax.dot_general(a, b, (((0,), (0,)), ((), ())), preferred_element_type=F32)


def rope_tables(places, head_size):
    half_dim = head_size // 2
    frequency = ROPE_BASE ** (-2.0 * jnp.arange(half_dim, dtype=F32) / head_size)
    angles = places.astype(F32)[:, None] * frequency[None, :]
    return (jnp.cos(angles)[:, None, :], jnp.sin(angles)[:, None, :])


def rotate(values, cosine, sine_table):
    half_dim = values.shape[-1] // 2
    first_half = values[..., :half_dim]
    second_half = values[..., half_dim:]
    return jnp.concatenate(
        [
            first_half * cosine - second_half * sine_table,
            second_half * cosine + first_half * sine_table,
        ],
        axis=-1,
    )


def rotate_back(values, cosine, sine_table):
    return rotate(values, cosine, -sine_table)


def rms_unit(values):
    factor = lax.rsqrt(jnp.mean(values * values, axis=-1, keepdims=True) + NORM_EPS)
    return (values * factor, factor)


def rms_backward(upstream, normed, factor, gain_row):
    scaled = upstream * (1.0 + gain_row)
    return factor * (scaled - normed * jnp.mean(scaled * normed, axis=-1, keepdims=True))


def pair_unit(pair):
    width = 2 * pair[0].shape[-1]
    total = sum(jnp.sum(v * v, axis=-1, keepdims=True) for v in pair)
    factor = lax.rsqrt(total / width + NORM_EPS)
    return (tuple(v * factor for v in pair), factor)


def pair_gain(units, gains):
    return tuple(u * (1.0 + g) for u, g in zip(units, gains))


def pair_back(upstream, units, factor, gains):
    width = 2 * units[0].shape[-1]
    scaled = tuple(e * (1.0 + g) for e, g in zip(upstream, gains))
    mean = sum(jnp.sum(s * u, axis=-1, keepdims=True) for s, u in zip(scaled, units)) / width
    return tuple(factor * (s - u * mean) for s, u in zip(scaled, units))


def gelu_parts(values):
    tangent = jnp.tanh(GELU_COEF * (values + 0.044715 * values * values * values))
    value = 0.5 * values * (1.0 + tangent)
    slope = 0.5 * (1.0 + tangent) + 0.5 * values * (1.0 - tangent * tangent) * GELU_COEF * (
        1.0 + 3.0 * 0.044715 * values * values
    )
    return (value, slope)


def visible(lo_ref, start, span, heads):
    rows = lax.broadcasted_iota(jnp.int32, (span, BLOCK), 0) + start
    queries = lax.broadcasted_iota(jnp.int32, (1, BLOCK), 1) + pl.program_id(0) * BLOCK
    seen = (rows >= lo_ref[...]) & (rows <= queries)
    return jnp.concatenate([seen] * heads, axis=1)


def stacked(ref, heads):
    width = ref.shape[1] // heads
    return jnp.concatenate([ref[:, h * width : (h + 1) * width] for h in range(heads)], axis=0)


def row_of(ref, heads):
    return jnp.concatenate([ref[h : h + 1, :] for h in range(heads)], axis=1)


def key_start(span):
    end = (pl.program_id(0) + 1) * BLOCK
    return pl.multiple_of(jnp.maximum(end - span, 0), BLOCK)


def attend_kernel(span, heads, q_ref, k_ref, vt_ref, lo_ref, out_ref, lse_ref):
    start = key_start(span)
    width = k_ref.shape[1]
    queries = stacked(q_ref, heads)
    scores = mm_nt(k_ref[pl.ds(start, span), :], queries)
    scores = jnp.where(visible(lo_ref, start, span, heads), scores, MASKED)
    top = jnp.max(scores, axis=0, keepdims=True)
    weights = jnp.exp(scores - top)
    total = jnp.sum(weights, axis=0, keepdims=True)
    result = mm(vt_ref[:, pl.ds(start, span)], weights.astype(HALF)) / total
    lse = top + jnp.log(total)
    for h in range(heads):
        part = slice(h * BLOCK, (h + 1) * BLOCK)
        out_ref[:, h * width : (h + 1) * width] = result[:, part].T.astype(HALF)
        lse_ref[h : h + 1, :] = lse[:, part]


def attend_back_kernel(
    span, heads, q_ref, k_ref, kt_ref, v_ref, do_ref, lo_ref, lse_ref, delta_ref,
    dq_ref, dk_ref, dv_ref,
):
    start = key_start(span)
    width = k_ref.shape[1]

    @pl.when(pl.program_id(0) == 0)
    def _():
        dk_ref[...] = jnp.zeros_like(dk_ref)
        dv_ref[...] = jnp.zeros_like(dv_ref)

    keys = pl.ds(start, span)
    queries = stacked(q_ref, heads)
    upstream = stacked(do_ref, heads)
    scores = mm_nt(k_ref[keys, :], queries)
    scores = jnp.where(visible(lo_ref, start, span, heads), scores, MASKED)
    weights = jnp.exp(scores - row_of(lse_ref, heads))
    dv_ref[keys, :] += mm(weights.astype(HALF), upstream)
    weight_grad = mm_nt(v_ref[keys, :], upstream)
    score_grad = (weights * (weight_grad - row_of(delta_ref, heads))).astype(HALF)
    dk_ref[keys, :] += mm(score_grad, queries)
    grad = mm(kt_ref[:, keys], score_grad)
    for h in range(heads):
        dq_ref[:, h * width : (h + 1) * width] = grad[:, h * BLOCK : (h + 1) * BLOCK].T


def kernel_params(count):
    return pltpu.CompilerParams(
        dimension_semantics=("arbitrary",), vmem_limit_bytes=48 * 1024 * 1024
    )


def full_spec(shape):
    return pl.BlockSpec(shape, lambda i: (0,) * len(shape))


def attend(q, k, v, lo):
    length, columns = q.shape
    width = k.shape[1]
    heads = columns // width
    span = min(WINDOW + BLOCK, length)
    rows = pl.BlockSpec((BLOCK, columns), lambda i: (i, 0))
    lane = lambda n: pl.BlockSpec((n, BLOCK), lambda i: (0, i))
    steps = length // BLOCK
    return pl.pallas_call(
        functools.partial(attend_kernel, span, heads),
        grid=(steps,),
        in_specs=[rows, full_spec(k.shape), full_spec((width, length)), lane(1)],
        out_specs=[rows, lane(heads)],
        out_shape=[
            jax.ShapeDtypeStruct(q.shape, HALF),
            jax.ShapeDtypeStruct((heads, length), F32),
        ],
        compiler_params=kernel_params(1),
        cost_estimate=pl.CostEstimate(
            flops=4 * steps * span * BLOCK * columns,
            bytes_accessed=4 * length * columns + 4 * length * width,
            transcendentals=steps * span * BLOCK * heads,
        ),
        name="attend",
    )(q, k, v.T, lo)


def attend_back(q, k, v, do, lo, lse, delta):
    length, columns = q.shape
    width = k.shape[1]
    heads = columns // width
    span = min(WINDOW + BLOCK, length)
    rows = pl.BlockSpec((BLOCK, columns), lambda i: (i, 0))
    lane = lambda n: pl.BlockSpec((n, BLOCK), lambda i: (0, i))
    steps = length // BLOCK
    return pl.pallas_call(
        functools.partial(attend_back_kernel, span, heads),
        grid=(steps,),
        in_specs=[
            rows, full_spec(k.shape), full_spec((width, length)), full_spec(v.shape), rows,
            lane(1), lane(heads), lane(heads),
        ],
        out_specs=[rows, full_spec(k.shape), full_spec(v.shape)],
        out_shape=[
            jax.ShapeDtypeStruct(q.shape, F32),
            jax.ShapeDtypeStruct(k.shape, F32),
            jax.ShapeDtypeStruct(v.shape, F32),
        ],
        compiler_params=kernel_params(1),
        cost_estimate=pl.CostEstimate(
            flops=10 * steps * span * BLOCK * columns,
            bytes_accessed=8 * length * columns + 14 * length * width,
            transcendentals=steps * span * BLOCK * heads,
        ),
        name="attend_back",
    )(q, k, k.T, v, do, lo, lse, delta)


def first_visible(segments):
    length = segments.shape[0]
    ids = jnp.arange(length, dtype=jnp.int32)
    begins = jnp.concatenate([jnp.ones((1,), bool), segments[1:] != segments[:-1]])
    starts = lax.cummax(jnp.where(begins, ids, 0), axis=0)
    return jnp.maximum(starts, ids - (WINDOW - 1))[None, :]


def adam_update(weight_shard, grad_shard, mean_shard, square_shard, decay):
    new_mean = BETA_ONE * mean_shard + (1.0 - BETA_ONE) * grad_shard
    new_square = BETA_TWO * square_shard + (1.0 - BETA_TWO) * grad_shard * grad_shard
    mean_hat = new_mean / (1.0 - BETA_ONE**STEP)
    square_hat = new_square / (1.0 - BETA_TWO**STEP)
    weight_value = weight_shard.astype(F32)
    updated = weight_value - LEARN_RATE * (
        mean_hat / (jnp.sqrt(square_hat) + ADAM_EPS) + decay * weight_value
    )
    return (updated, new_mean, new_square)


def shards(
    n_dp,
    hidden_in,
    segment_ids,
    positions,
    cotangent,
    query_weight,
    key_projection,
    value_projection,
    output_weight,
    gate_weight,
    upward_weight,
    down_weight,
    norm_gains,
    head_gains,
    query_mean,
    query_square,
    key_first_moment,
    key_second_moment,
    value_first_moment,
    value_second_moment,
    output_mean,
    output_square,
    gate_mean,
    gate_square,
    upward_mean,
    upward_square,
    down_mean,
    down_square,
    norms_mean,
    norms_square,
    heads_mean,
    heads_square,
):
    tokens, model = hidden_in.shape
    share = model // n_dp
    quarter = tokens // 4
    half = model // 2
    spot = lax.axis_index("dp")
    parity = spot % 2
    place = lax.axis_index("tensor")
    core = place % 2
    row = place // 2
    outer = [[2 * i + p for i in range(n_dp // 2)] for p in range(2)]
    twins = [(i, i ^ 1) for i in range(n_dp)]

    def to_twin(x):
        return lax.ppermute(x, "dp", twins)

    def to_core(x):
        return lax.ppermute(x, "tensor", [(i, i ^ 1) for i in range(4)])

    def to_row(x):
        return lax.ppermute(x, "tensor", [(i, i ^ 2) for i in range(4)])

    def split_columns(x):
        parts = [x[:, i * share : (i + 1) * share] for i in range(n_dp)]
        even = jnp.concatenate(parts[0::2], axis=1)
        odd = jnp.concatenate(parts[1::2], axis=1)
        return (jnp.where(parity == 0, even, odd), jnp.where(parity == 0, odd, even))

    def join_columns(pair):
        even = jnp.where(parity == 0, pair[0], pair[1])
        odd = jnp.where(parity == 0, pair[1], pair[0])
        parts = []
        for i in range(n_dp // 2):
            parts.append(even[:, i * share : (i + 1) * share])
            parts.append(odd[:, i * share : (i + 1) * share])
        return jnp.concatenate(parts, axis=1)

    order = [
        (core * 2 + row) * quarter,
        (core * 2 + 1 - row) * quarter,
        ((1 - core) * 2 + row) * quarter,
        ((1 - core) * 2 + 1 - row) * quarter,
    ]

    def rows_at(x, at):
        return lax.dynamic_slice_in_dim(x, at, quarter, 0)

    def own_order(x):
        return jnp.concatenate([rows_at(x, at) for at in order], axis=0)

    def place_rows(pieces):
        out = jnp.zeros((tokens,) + pieces[0].shape[1:], pieces[0].dtype)
        for piece, at in zip(pieces, order):
            out = lax.dynamic_update_slice_in_dim(out, piece, at, 0)
        return out

    def reduce_rows(product):
        def one(which):
            far = product(which, 3 * quarter, 4 * quarter).astype(HALF)
            far_in = to_core(far)
            near = product(which, quarter, 2 * quarter) + far_in.astype(F32)
            near_in = to_row(near.astype(HALF))
            side = to_core(product(which, 2 * quarter, 3 * quarter).astype(HALF))
            mine = product(which, 0, quarter) + side.astype(F32)
            return mine + near_in.astype(F32)

        return (one(0), one(1))

    def spread_pieces(x):
        across = to_row(x)
        return [x, across, to_core(x), to_core(across)]

    def spread_rows(x):
        return jnp.concatenate(spread_pieces(x), axis=0)

    def gather_model(shard, chunks):
        width = shard.shape[1] // chunks
        found = []
        for j in range(chunks):
            piece = shard[:, j * width : (j + 1) * width]
            mine = lax.all_gather(piece, "dp", axis=0, tiled=True, axis_index_groups=outer)
            found.append((mine, to_twin(mine)))
        return found

    def scatter_model(make, chunks):
        found = []
        for j in range(chunks):
            other = to_twin(make(1, j).astype(HALF))
            total = (make(0, j) + other.astype(F32)).astype(HALF)
            found.append(
                lax.psum_scatter(
                    total, "dp", scatter_dimension=0, tiled=True, axis_index_groups=outer
                )
            )
        return jnp.concatenate(found, axis=1)

    q_cols = query_weight.shape[1]
    kv_cols = key_projection.shape[1]
    gain_block = jnp.concatenate(
        [
            norm_gains.T,
            jnp.pad(head_gains.T, ((0, share - head_gains.shape[1]), (0, 0))),
            jnp.zeros((share, 128 - 6), HALF),
        ],
        axis=1,
    )
    front_shard = jnp.concatenate(
        [query_weight, key_projection, value_projection, gain_block], axis=1
    )
    front = gather_model(front_shard, 1)[0]
    back = gather_model(output_weight.T, 1)[0]
    gates = gather_model(gate_weight, CHUNKS)
    upwards = gather_model(upward_weight, CHUNKS)
    downs = gather_model(down_weight.T, CHUNKS)

    front_width = q_cols + 2 * kv_cols
    gains = tuple(f[:, front_width : front_width + 4].T.astype(F32) for f in front)
    gain = [tuple(g[i : i + 1, :] for g in gains) for i in range(4)]
    head_width = head_gains.shape[1]
    head_parts = [
        f[:, front_width + 4 : front_width + 6]
        .reshape(n_dp // 2, share, 2)[:, :head_width, :]
        .astype(F32)
        for f in front
    ]
    head_even = jnp.where(parity == 0, head_parts[0], head_parts[1])
    head_odd = jnp.where(parity == 0, head_parts[1], head_parts[0])
    head_gain = jnp.stack([head_even, head_odd], axis=1).reshape(n_dp * head_width, 2).T
    front_w = tuple(f[:, :front_width] for f in front)

    rows_pair = split_columns(hidden_in)
    rows_f32 = tuple(r.astype(F32) for r in rows_pair)
    unit_all, _ = pair_unit(rows_f32)
    attn_in = tuple(v.astype(HALF) for v in pair_gain(unit_all, gain[0]))
    own_in = tuple(rows_at(r, order[0]).astype(F32) for r in rows_pair)
    unit_one, factor_one = pair_unit(own_in)
    projected = mm(attn_in[0], front_w[0]) + mm(attn_in[1], front_w[1])
    places = positions[0]
    cosine, sine_table = rope_tables(places, HEAD_WIDTH)
    scale = HEAD_WIDTH ** (-0.5)
    query_unit, query_factor = rms_unit(projected[:, :q_cols].reshape(tokens, -1, HEAD_WIDTH))
    key_unit, key_factor = rms_unit(
        projected[:, q_cols : q_cols + kv_cols].reshape(tokens, -1, HEAD_WIDTH)
    )
    value_heads = projected[:, q_cols + kv_cols :].astype(HALF)
    query_rot = rotate(query_unit * (1.0 + head_gain[0]), cosine, sine_table).astype(HALF)
    key_rot = rotate(key_unit * (1.0 + head_gain[1]), cosine, sine_table).astype(HALF)
    query_scaled = (query_rot * HALF(scale)).reshape(tokens, q_cols)
    key_heads = key_rot.reshape(tokens, kv_cols)
    lo = first_visible(segment_ids[0])
    attended, lse = attend(query_scaled, key_heads, value_heads, lo)
    attended_own = own_order(attended)
    attn_sum = reduce_rows(lambda w, a, b: mm_nt(attended_own[a:b], back[w]))
    unit_two, factor_two = pair_unit(attn_sum)
    middle = tuple(x + y for x, y in zip(own_in, pair_gain(unit_two, gain[1])))
    unit_three, factor_three = pair_unit(middle)
    ffn_in = tuple(
        spread_rows(v.astype(HALF)) for v in pair_gain(unit_three, gain[2])
    )

    mixed, kept_value, kept_slope = [], [], []
    for j in range(CHUNKS):
        gate_pre = mm(ffn_in[0], gates[j][0]) + mm(ffn_in[1], gates[j][1])
        upward_pre = mm(ffn_in[0], upwards[j][0]) + mm(ffn_in[1], upwards[j][1])
        value, slope = gelu_parts(gate_pre)
        mixed.append((value * upward_pre).astype(HALF))
        kept_value.append(value.astype(HALF))
        kept_slope.append((slope * upward_pre).astype(HALF))

    def down_product(which, first, last):
        return sum(mm_nt(mixed[j][first:last], downs[j][which]) for j in range(CHUNKS))

    ffn_sum = reduce_rows(down_product)
    unit_four, factor_four = pair_unit(ffn_sum)
    block_own = join_columns(
        tuple((x + y).astype(HALF) for x, y in zip(middle, pair_gain(unit_four, gain[3])))
    )
    block_output = place_rows(spread_pieces(block_own))

    upstream = tuple(c.astype(F32) for c in split_columns(rows_at(cotangent, order[0])))
    gain_four = tuple(jnp.sum(e * u, axis=0) for e, u in zip(upstream, unit_four))
    ffn_grad = tuple(
        spread_rows(v.astype(HALF)) for v in pair_back(upstream, unit_four, factor_four, gain[3])
    )
    down_wgrad = scatter_model(lambda w, j: mm_tn(ffn_grad[w], mixed[j]), CHUNKS)
    gate_back, upward_back = [], []
    for j in range(CHUNKS):
        hidden_grad = mm(ffn_grad[0], downs[j][0]) + mm(ffn_grad[1], downs[j][1])
        gate_back.append((hidden_grad * kept_slope[j].astype(F32)).astype(HALF))
        upward_back.append((hidden_grad * kept_value[j].astype(F32)).astype(HALF))

    def back_product(which, first, last):
        return sum(
            mm_nt(gate_back[j][first:last], gates[j][which])
            + mm_nt(upward_back[j][first:last], upwards[j][which])
            for j in range(CHUNKS)
        )

    ffn_in_grad = reduce_rows(back_product)
    gate_wgrad = scatter_model(lambda w, j: mm_tn(ffn_in[w], gate_back[j]), CHUNKS)
    upward_wgrad = scatter_model(lambda w, j: mm_tn(ffn_in[w], upward_back[j]), CHUNKS)
    gain_three = tuple(jnp.sum(e * u, axis=0) for e, u in zip(ffn_in_grad, unit_three))
    middle_grad = tuple(
        x + y
        for x, y in zip(upstream, pair_back(ffn_in_grad, unit_three, factor_three, gain[2]))
    )
    gain_two = tuple(jnp.sum(e * u, axis=0) for e, u in zip(middle_grad, unit_two))
    attn_grad = tuple(
        spread_rows(v.astype(HALF)) for v in pair_back(middle_grad, unit_two, factor_two, gain[1])
    )

    attended_grad = mm(attn_grad[0], back[0]) + mm(attn_grad[1], back[1])
    output_wgrad = scatter_model(lambda w, j: mm_tn(attn_grad[w], attended_own), 1)
    delta = jnp.sum(
        (attended_grad * attended_own.astype(F32)).reshape(tokens, -1, HEAD_WIDTH), axis=-1
    )
    grad_natural = place_rows(jnp.split(attended_grad.astype(HALF), 4, axis=0))
    delta_natural = place_rows(jnp.split(delta, 4, axis=0)).T
    query_grad, key_grad, value_grad = attend_back(
        query_scaled, key_heads, value_heads, grad_natural, lo, lse, delta_natural
    )
    query_grad = (query_grad * scale).reshape(query_unit.shape)
    query_turned = rotate_back(query_grad, cosine, sine_table)
    key_turned = rotate_back(key_grad.reshape(key_unit.shape), cosine, sine_table)
    head_part = jnp.stack(
        [
            jnp.sum(query_turned * query_unit, axis=(0, 1)),
            jnp.sum(key_turned * key_unit, axis=(0, 1)),
        ]
    )
    query_flat = rms_backward(query_turned, query_unit, query_factor, head_gain[0])
    key_flat = rms_backward(key_turned, key_unit, key_factor, head_gain[1])
    front_grad = jnp.concatenate(
        [
            query_flat.astype(HALF).reshape(tokens, q_cols),
            key_flat.astype(HALF).reshape(tokens, kv_cols),
            value_grad.astype(HALF),
        ],
        axis=1,
    )
    front_wgrad = scatter_model(lambda w, j: mm_tn(attn_in[w], front_grad), 1)
    front_own = own_order(front_grad)
    attn_in_grad = reduce_rows(lambda w, a, b: mm_nt(front_own[a:b], front_w[w]))
    gain_one = tuple(jnp.sum(e * u, axis=0) for e, u in zip(attn_in_grad, unit_one))
    input_own = join_columns(
        tuple(
            (x + y).astype(HALF)
            for x, y in zip(middle_grad, pair_back(attn_in_grad, unit_one, factor_one, gain[0]))
        )
    )
    input_grad = place_rows([p.astype(F32) for p in spread_pieces(input_own)])

    gain_rows = join_columns(
        tuple(jnp.stack([a, b, c, d]) for a, b, c, d in zip(gain_one, gain_two, gain_three, gain_four))
    )
    flat = jnp.concatenate([gain_rows.reshape(-1), head_part.reshape(-1)])
    flat = lax.psum(flat, ("dp", "tensor"))
    gain_total = flat[: 4 * model].reshape(4, model)
    head_total = flat[4 * model :].reshape(2, -1)
    norms_grad = lax.dynamic_slice_in_dim(gain_total, spot * share, share, 1)
    heads_grad = lax.dynamic_slice_in_dim(head_total, spot * head_width, head_width, 1)

    grad_shards = (
        front_wgrad[:, :q_cols].astype(F32),
        front_wgrad[:, q_cols : q_cols + kv_cols].astype(F32),
        front_wgrad[:, q_cols + kv_cols :].astype(F32),
        output_wgrad.T.astype(F32),
        gate_wgrad.astype(F32),
        upward_wgrad.astype(F32),
        down_wgrad.T.astype(F32),
        norms_grad,
        heads_grad,
    )
    params = (
        query_weight,
        key_projection,
        value_projection,
        output_weight,
        gate_weight,
        upward_weight,
        down_weight,
        norm_gains,
        head_gains,
    )
    means = (
        query_mean,
        key_first_moment,
        value_first_moment,
        output_mean,
        gate_mean,
        upward_mean,
        down_mean,
        norms_mean,
        heads_mean,
    )
    squares = (
        query_square,
        key_second_moment,
        value_second_moment,
        output_square,
        gate_square,
        upward_square,
        down_square,
        norms_square,
        heads_square,
    )
    decays = (DECAY_RATE,) * 7 + (0.0, 0.0)
    results = [
        adam_update(param, grad_item, mean_item, square_item, decay)
        for param, grad_item, mean_item, square_item, decay in zip(
            params, grad_shards, means, squares, decays
        )
    ]
    updated = tuple((item[0] for item in results))
    new_means = tuple((item[1] for item in results))
    new_squares = tuple((item[2] for item in results))
    return (block_output, input_grad) + grad_shards + updated + new_means + new_squares


def solution(mesh):
    in_specs = (
        P("dp", None),
        P("dp", None),
        P("dp", None),
        P("dp", None),
        P("dp", "tensor"),
        P("dp", "tensor"),
        P("dp", "tensor"),
        P("tensor", "dp"),
        P("dp", "tensor"),
        P("dp", "tensor"),
        P("tensor", "dp"),
        P(None, "dp"),
        P(None, "dp"),
        P("dp", "tensor"),
        P("dp", "tensor"),
        P("dp", "tensor"),
        P("dp", "tensor"),
        P("dp", "tensor"),
        P("dp", "tensor"),
        P("tensor", "dp"),
        P("tensor", "dp"),
        P("dp", "tensor"),
        P("dp", "tensor"),
        P("dp", "tensor"),
        P("dp", "tensor"),
        P("tensor", "dp"),
        P("tensor", "dp"),
        P(None, "dp"),
        P(None, "dp"),
        P(None, "dp"),
        P(None, "dp"),
    )
    out_specs = (
        P("dp", None),
        P("dp", None),
        P("dp", "tensor"),
        P("dp", "tensor"),
        P("dp", "tensor"),
        P("tensor", "dp"),
        P("dp", "tensor"),
        P("dp", "tensor"),
        P("tensor", "dp"),
        P(None, "dp"),
        P(None, "dp"),
        P("dp", "tensor"),
        P("dp", "tensor"),
        P("dp", "tensor"),
        P("tensor", "dp"),
        P("dp", "tensor"),
        P("dp", "tensor"),
        P("tensor", "dp"),
        P(None, "dp"),
        P(None, "dp"),
        P("dp", "tensor"),
        P("dp", "tensor"),
        P("dp", "tensor"),
        P("tensor", "dp"),
        P("dp", "tensor"),
        P("dp", "tensor"),
        P("tensor", "dp"),
        P(None, "dp"),
        P(None, "dp"),
        P("dp", "tensor"),
        P("dp", "tensor"),
        P("dp", "tensor"),
        P("tensor", "dp"),
        P("dp", "tensor"),
        P("dp", "tensor"),
        P("tensor", "dp"),
        P(None, "dp"),
        P(None, "dp"),
    )
    return jax.shard_map(functools.partial(shards, mesh.shape["dp"]), mesh=mesh, in_specs=in_specs, out_specs=out_specs, check_vma=False)
```

```python
import functools

import jax
import jax.numpy as jnp
from jax import lax
from jax.experimental import pallas as pl
from jax.experimental.pallas import tpu as pltpu
from jax.sharding import PartitionSpec as P

HEAD_WIDTH = 256
WINDOW = 1024
STEP = 4
CHUNKS = 2
BLOCK = 256

NORM_EPS = 1e-06
BETA_ONE = 0.9
BETA_TWO = 0.999
ADAM_EPS = 1e-08
LEARN_RATE = 0.01
DECAY_RATE = 0.1
ROPE_BASE = 10000.0
GELU_COEF = 0.7978845608028654
MASKED = -1e30


DP = "dp"
TENSOR = "tensor"
F32 = jnp.float32
HALF = jnp.bfloat16


def contract(a, b, form):
    dims = ((0 if form[0] == "t" else 1,), (1 if form[1] == "t" else 0,))
    return lax.dot_general(a, b, (dims, ((), ())), preferred_element_type=F32)


def mm(a, b):
    return contract(a, b, "nn")


def mm_nt(a, b):
    return contract(a, b, "nt")


def fused_dots(grid, terms, extras, outs, finish):
    arrays, specs, plan, flops = [], [], [], 0
    steps = 1
    for size in grid:
        steps *= size
    for left, left_spec, right, right_spec, form, slot in terms:
        plan.append((len(arrays), form, slot))
        arrays += [left, right]
        specs += [left_spec, right_spec]
        shape = [n for n in left_spec.block_shape if n is not None]
        other = [n for n in right_spec.block_shape if n is not None]
        columns = other[0] if form[1] == "t" else other[1]
        flops += 2 * steps * shape[0] * shape[1] * columns
    base = len(arrays)
    for extra, spec in extras:
        arrays.append(extra)
        specs.append(spec)
    count = len(arrays)
    slots = 1 + max(slot for _, _, slot in plan)

    def kernel(*refs):
        sums = [None] * slots
        for at, form, slot in plan:
            product = contract(refs[at][...], refs[at + 1][...], form)
            sums[slot] = product if sums[slot] is None else sums[slot] + product
        finish(sums, refs[base:count], refs[count:])

    moved = sum(a.size * a.dtype.itemsize for a in {id(a): a for a in arrays}.values())
    return pl.pallas_call(
        kernel,
        grid=grid,
        in_specs=specs,
        out_specs=[spec for _, _, spec in outs],
        out_shape=[jax.ShapeDtypeStruct(shape, dtype) for shape, dtype, _ in outs],
        compiler_params=pltpu.CompilerParams(
            dimension_semantics=("arbitrary",) * len(grid),
            vmem_limit_bytes=56 * 1024 * 1024,
        ),
        cost_estimate=pl.CostEstimate(flops=flops, bytes_accessed=moved, transcendentals=0),
    )(*arrays)


def rope_tables(places, head_size):
    half_dim = head_size // 2
    frequency = ROPE_BASE ** (-2.0 * jnp.arange(half_dim, dtype=F32) / head_size)
    angles = places.astype(F32)[:, None] * frequency[None, :]
    return (jnp.cos(angles), jnp.sin(angles))


def rotate(values, cosine, sine_table):
    half_dim = values.shape[-1] // 2
    first_half = values[..., :half_dim]
    second_half = values[..., half_dim:]
    return jnp.concatenate(
        [
            first_half * cosine - second_half * sine_table,
            second_half * cosine + first_half * sine_table,
        ],
        axis=-1,
    )


def rms_unit(values):
    factor = lax.rsqrt(jnp.mean(values * values, axis=-1, keepdims=True) + NORM_EPS)
    return (values * factor, factor)


def rms_backward(upstream, normed, factor, gain_row):
    scaled = upstream * (1.0 + gain_row)
    return factor * (scaled - normed * jnp.mean(scaled * normed, axis=-1, keepdims=True))


def gelu_parts(values):
    tangent = jnp.tanh(GELU_COEF * (values + 0.044715 * values * values * values))
    value = 0.5 * values * (1.0 + tangent)
    slope = 0.5 * (1.0 + tangent) + 0.5 * values * (1.0 - tangent * tangent) * GELU_COEF * (
        1.0 + 3.0 * 0.044715 * values * values
    )
    return (value, slope)


def row_sum(values, width):
    total = sum(jnp.sum(v, axis=-1, keepdims=True) for v in values)
    return total / width


def unit_of(values, width):
    factor = lax.rsqrt(row_sum([v * v for v in values], width) + NORM_EPS)
    return ([v * factor for v in values], factor)


def back_of(upstream, units, factor, gains, width):
    scaled = [e * (1.0 + g) for e, g in zip(upstream, gains)]
    mean = row_sum([s * u for s, u in zip(scaled, units)], width)
    return [factor * (s - u * mean) for s, u in zip(scaled, units)]


def halves(ref):
    return [ref[w].astype(F32) for w in range(ref.shape[0])]


def put(ref, pair):
    for w, value in enumerate(pair):
        ref[w] = value.astype(ref.dtype)


def put_sum(ref, upstream, units):
    @pl.when(pl.program_id(0) == 0)
    def _():
        ref[...] = jnp.zeros_like(ref)

    for w, (e, u) in enumerate(zip(upstream, units)):
        ref[w] += jnp.sum(e * u, axis=0, keepdims=True)


def glue(inputs, gains, outs, sums, body):
    rows, half = inputs[0].shape[1:]
    tile = min(64, rows)
    block = lambda n: pl.BlockSpec((n, tile, half), lambda i: (0, i, 0))
    still = pl.BlockSpec((2, 1, half), lambda i: (0, 0, 0))
    return pl.pallas_call(
        body,
        grid=(rows // tile,),
        in_specs=[block(x.shape[0]) for x in inputs] + [still] * len(gains),
        out_specs=[block(2)] * len(outs) + [still] * sums,
        out_shape=[jax.ShapeDtypeStruct((2, rows, half), dtype) for dtype in outs]
        + [jax.ShapeDtypeStruct((2, 1, half), F32)] * sums,
        compiler_params=kernel_params(),
        cost_estimate=pl.CostEstimate(
            flops=64 * rows * half, bytes_accessed=40 * rows * half, transcendentals=0
        ),
    )(*inputs, *gains)


def glue_one(mine, near, own, gain_two, gain_three, sum_ref, middle_ref, ffn_ref):
    width = 2 * mine.shape[2]
    total = [a + b for a, b in zip(halves(mine), halves(near))]
    units, _ = unit_of(total, width)
    middle = [x + u * (1.0 + g) for x, u, g in zip(halves(own), units, halves(gain_two))]
    units, _ = unit_of(middle, width)
    put(sum_ref, total)
    put(middle_ref, middle)
    put(ffn_ref, [u * (1.0 + g) for u, g in zip(units, halves(gain_three))])


def glue_two(
    mine_a, near_a, mine_b, near_b, middle, upstream, gain, block_ref, grad_ref, sum_ref
):
    width = 2 * middle.shape[2]
    total = [mine_a[0] + near_a[0].astype(F32), mine_b[0] + near_b[0].astype(F32)]
    units, factor = unit_of(total, width)
    gains = halves(gain)
    errors = halves(upstream)
    put(block_ref, [x + u * (1.0 + g) for x, u, g in zip(halves(middle), units, gains)])
    put(grad_ref, back_of(errors, units, factor, gains, width))
    put_sum(sum_ref, errors, units)


def glue_three(
    mine, near, middle, upstream, attn_sum, gain_two, gain_three,
    grad_ref, attn_ref, sum_three_ref, sum_two_ref,
):
    width = 2 * middle.shape[2]
    errors = [a + b for a, b in zip(halves(mine), halves(near))]
    units, factor = unit_of(halves(middle), width)
    back = back_of(errors, units, factor, halves(gain_three), width)
    put_sum(sum_three_ref, errors, units)
    grads = [x + y for x, y in zip(halves(upstream), back)]
    put(grad_ref, grads)
    units, factor = unit_of(halves(attn_sum), width)
    put_sum(sum_two_ref, grads, units)
    put(attn_ref, back_of(grads, units, factor, halves(gain_two), width))


def glue_four(mine, near, own, middle_grad, gain_one, out_ref, sum_ref):
    width = 2 * own.shape[2]
    errors = [a + b for a, b in zip(halves(mine), halves(near))]
    units, factor = unit_of(halves(own), width)
    back = back_of(errors, units, factor, halves(gain_one), width)
    put(out_ref, [x + y for x, y in zip(halves(middle_grad), back)])
    put_sum(sum_ref, errors, units)


def take_piece(refs, per, store):
    for k, ref in enumerate(refs):

        @pl.when(pl.program_id(0) // per == k)
        def _(ref=ref):
            store(ref)


def piece_index(per, k):
    return lambda i: jnp.clip(i - k * per, 0, per - 1)


def place_rows(pieces, order, dtype):
    rows, width = pieces[0].shape
    tile = min(128, rows)
    per = rows // tile

    def kernel(order_ref, *refs):
        def store(ref):
            refs[-1][...] = ref[...].astype(dtype)

        take_piece(refs[:-1], per, store)

    specs = [
        pl.BlockSpec((tile, width), lambda i, o, k=k: (piece_index(per, k)(i), 0))
        for k in range(len(pieces))
    ]
    return pl.pallas_call(
        kernel,
        grid_spec=pltpu.PrefetchScalarGridSpec(
            num_scalar_prefetch=1,
            grid=(len(pieces) * per,),
            in_specs=specs,
            out_specs=pl.BlockSpec((tile, width), lambda i, o: (o[i // per] * per + i % per, 0)),
        ),
        out_shape=jax.ShapeDtypeStruct((len(pieces) * rows, width), dtype),
        compiler_params=kernel_params(),
        cost_estimate=pl.CostEstimate(flops=0, bytes_accessed=24 * rows * width, transcendentals=0),
    )(order, *pieces)


def all_rows(pieces, weights, width, extras, outs, finish, first=0, order=None):
    rows, half = pieces[0].shape[1:]
    tile = min(256, rows)
    per = rows // tile
    steps = len(pieces) * per
    count = len(pieces)
    slots = len(weights)

    def kernel(*refs):
        if order is not None:
            refs = refs[1:]
        flat = refs[count : count + 2 * slots]
        rest = refs[count + 2 * slots :]
        if count > 1:
            rest, left = rest[:-1], rest[-1]

            def store(ref):
                left[...] = ref[...]

            take_piece(refs[:count], per, store)
        else:
            left = refs[0]
        sums = [
            contract(left[0], flat[2 * s][...], "nn") + contract(left[1], flat[2 * s + 1][...], "nn")
            for s in range(slots)
        ]
        finish(sums, rest[: len(extras)], rest[len(extras) :])

    specs = [
        pl.BlockSpec((2, tile, half), lambda i, *o, k=k: (0, piece_index(per, k)(i), 0))
        for k in range(count)
    ]
    for pair in weights:
        columns = min(pair[0].shape[1], width)
        specs += [pl.BlockSpec((half, columns), lambda i, *o: (0, 0))] * 2
    skip = first * (rows // tile)
    specs += [pl.BlockSpec((tile, width), lambda i, *o: (skip + i, 0))] * len(extras)
    if order is None:
        target = pl.BlockSpec((tile, width), lambda i: (i, 0))
    else:
        target = pl.BlockSpec((tile, width), lambda i, o: (o[i // per] * per + i % per, 0))
    scratch = [pltpu.VMEM((2, tile, half), HALF)] if count > 1 else []
    arrays = list(pieces) + [w for pair in weights for w in pair] + list(extras)
    return pl.pallas_call(
        kernel,
        grid_spec=pltpu.PrefetchScalarGridSpec(
            num_scalar_prefetch=0 if order is None else 1,
            grid=(steps,),
            in_specs=specs,
            out_specs=[target] * len(outs),
            scratch_shapes=scratch,
        ),
        out_shape=[jax.ShapeDtypeStruct((steps * tile, width), dtype) for dtype in outs],
        compiler_params=pltpu.CompilerParams(
            dimension_semantics=("arbitrary",), vmem_limit_bytes=56 * 1024 * 1024
        ),
        cost_estimate=pl.CostEstimate(
            flops=4 * steps * tile * half * sum(pair[0].shape[1] for pair in weights),
            bytes_accessed=sum(a.size * a.dtype.itemsize for a in arrays),
            transcendentals=0,
        ),
    )(*([] if order is None else [order]), *arrays)


def visible(lo_ref, start, span, heads):
    rows = lax.broadcasted_iota(jnp.int32, (span, BLOCK), 0) + start
    queries = lax.broadcasted_iota(jnp.int32, (1, BLOCK), 1) + pl.program_id(0) * BLOCK
    seen = (rows >= lo_ref[...]) & (rows <= queries)
    return jnp.concatenate([seen] * heads, axis=1)


def stacked(ref, heads):
    width = ref.shape[1] // heads
    return jnp.concatenate([ref[:, h * width : (h + 1) * width] for h in range(heads)], axis=0)


def row_of(ref, heads):
    return jnp.concatenate([ref[h : h + 1, :] for h in range(heads)], axis=1)


def key_start(span):
    end = (pl.program_id(0) + 1) * BLOCK
    return pl.multiple_of(jnp.maximum(end - span, 0), BLOCK)


def attend_kernel(span, heads, q_ref, k_ref, vt_ref, lo_ref, out_ref, lse_ref):
    start = key_start(span)
    width = k_ref.shape[1]
    queries = stacked(q_ref, heads)
    scores = mm_nt(k_ref[pl.ds(start, span), :], queries)
    scores = jnp.where(visible(lo_ref, start, span, heads), scores, MASKED)
    top = jnp.max(scores, axis=0, keepdims=True)
    weights = jnp.exp(scores - top)
    total = jnp.sum(weights, axis=0, keepdims=True)
    result = mm(vt_ref[:, pl.ds(start, span)], weights.astype(HALF)) / total
    lse = top + jnp.log(total)
    for h in range(heads):
        part = slice(h * BLOCK, (h + 1) * BLOCK)
        out_ref[:, h * width : (h + 1) * width] = result[:, part].T.astype(HALF)
        lse_ref[h : h + 1, :] = lse[:, part]


def attend_back_kernel(
    span, heads, q_ref, k_ref, kt_ref, v_ref, do_ref, lo_ref, lse_ref, out_ref,
    dq_ref, dk_ref, dv_ref,
):
    start = key_start(span)
    width = k_ref.shape[1]

    @pl.when(pl.program_id(0) == 0)
    def _():
        dk_ref[...] = jnp.zeros_like(dk_ref)
        dv_ref[...] = jnp.zeros_like(dv_ref)

    keys = pl.ds(start, span)
    queries = stacked(q_ref, heads)
    upstream = stacked(do_ref, heads)
    scores = mm_nt(k_ref[keys, :], queries)
    scores = jnp.where(visible(lo_ref, start, span, heads), scores, MASKED)
    weights = jnp.exp(scores - row_of(lse_ref, heads))
    dv_ref[keys, :] += mm(weights.astype(HALF), upstream)
    weight_grad = mm_nt(v_ref[keys, :], upstream)
    pull = upstream.astype(F32) * stacked(out_ref, heads).astype(F32)
    delta = jnp.sum(pull.T, axis=0, keepdims=True)
    score_grad = (weights * (weight_grad - delta)).astype(HALF)
    dk_ref[keys, :] += mm(score_grad, queries)
    grad = mm(kt_ref[:, keys], score_grad)
    for h in range(heads):
        dq_ref[:, h * width : (h + 1) * width] = grad[:, h * BLOCK : (h + 1) * BLOCK].T


def kernel_params():
    return pltpu.CompilerParams(
        dimension_semantics=("arbitrary",), vmem_limit_bytes=48 * 1024 * 1024
    )


def full_spec(shape):
    return pl.BlockSpec(shape, lambda i: (0,) * len(shape))


def attend(q, k, v, lo):
    length, columns = q.shape
    width = k.shape[1]
    heads = columns // width
    span = min(WINDOW + BLOCK, length)
    rows = pl.BlockSpec((BLOCK, columns), lambda i: (i, 0))
    lane = lambda n: pl.BlockSpec((n, BLOCK), lambda i: (0, i))
    steps = length // BLOCK
    return pl.pallas_call(
        functools.partial(attend_kernel, span, heads),
        grid=(steps,),
        in_specs=[rows, full_spec(k.shape), full_spec((width, length)), lane(1)],
        out_specs=[rows, lane(heads)],
        out_shape=[
            jax.ShapeDtypeStruct(q.shape, HALF),
            jax.ShapeDtypeStruct((heads, length), F32),
        ],
        compiler_params=kernel_params(),
        cost_estimate=pl.CostEstimate(
            flops=4 * steps * span * BLOCK * columns,
            bytes_accessed=4 * length * columns + 4 * length * width,
            transcendentals=steps * span * BLOCK * heads,
        ),
        name="attend",
    )(q, k, v.T, lo)


def attend_back(q, k, v, do, lo, lse, out):
    length, columns = q.shape
    width = k.shape[1]
    heads = columns // width
    span = min(WINDOW + BLOCK, length)
    rows = pl.BlockSpec((BLOCK, columns), lambda i: (i, 0))
    lane = lambda n: pl.BlockSpec((n, BLOCK), lambda i: (0, i))
    steps = length // BLOCK
    return pl.pallas_call(
        functools.partial(attend_back_kernel, span, heads),
        grid=(steps,),
        in_specs=[
            rows, full_spec(k.shape), full_spec((width, length)), full_spec(v.shape), rows,
            lane(1), lane(heads), rows,
        ],
        out_specs=[rows, full_spec(k.shape), full_spec(v.shape)],
        out_shape=[
            jax.ShapeDtypeStruct(q.shape, F32),
            jax.ShapeDtypeStruct(k.shape, F32),
            jax.ShapeDtypeStruct(v.shape, F32),
        ],
        compiler_params=kernel_params(),
        cost_estimate=pl.CostEstimate(
            flops=10 * steps * span * BLOCK * columns,
            bytes_accessed=8 * length * columns + 14 * length * width,
            transcendentals=steps * span * BLOCK * heads,
        ),
        name="attend_back",
    )(q, k, k.T, v, do, lo, lse, out)


def first_visible(segments):
    length = segments.shape[0]
    ids = jnp.arange(length, dtype=jnp.int32)
    begins = jnp.concatenate([jnp.ones((1,), bool), segments[1:] != segments[:-1]])
    starts = lax.cummax(jnp.where(begins, ids, 0), axis=0)
    return jnp.maximum(starts, ids - (WINDOW - 1))[None, :]


def adam_update(weight_shard, grad_shard, mean_shard, square_shard, decay):
    new_mean = BETA_ONE * mean_shard + (1.0 - BETA_ONE) * grad_shard
    new_square = BETA_TWO * square_shard + (1.0 - BETA_TWO) * grad_shard * grad_shard
    mean_hat = new_mean / (1.0 - BETA_ONE**STEP)
    square_hat = new_square / (1.0 - BETA_TWO**STEP)
    weight_value = weight_shard.astype(F32)
    updated = weight_value - LEARN_RATE * (
        mean_hat / (jnp.sqrt(square_hat) + ADAM_EPS) + decay * weight_value
    )
    return (updated, new_mean, new_square)


def step(
    n_dp,
    hidden_in,
    segment_ids,
    positions,
    cotangent,
    query_weight,
    key_projection,
    value_projection,
    output_weight,
    gate_weight,
    upward_weight,
    down_weight,
    norm_gains,
    head_gains,
    query_mean,
    query_square,
    key_first_moment,
    key_second_moment,
    value_first_moment,
    value_second_moment,
    output_mean,
    output_square,
    gate_mean,
    gate_square,
    upward_mean,
    upward_square,
    down_mean,
    down_square,
    norms_mean,
    norms_square,
    heads_mean,
    heads_square,
):
    tokens, model = hidden_in.shape
    share = model // n_dp
    quarter = tokens // 4
    half = model // 2
    spot = lax.axis_index(DP)
    parity = spot % 2
    place = lax.axis_index(TENSOR)
    core = place % 2
    row = place // 2
    outer = [[2 * i + p for i in range(n_dp // 2)] for p in range(2)]
    twins = [(i, i ^ 1) for i in range(n_dp)]

    def to_twin(x):
        return lax.ppermute(x, DP, twins)

    def to_core(x):
        return lax.ppermute(x, TENSOR, [(i, i ^ 1) for i in range(4)])

    def to_row(x):
        return lax.ppermute(x, TENSOR, [(i, i ^ 2) for i in range(4)])

    def split_columns(x):
        parts = [x[:, i * share : (i + 1) * share] for i in range(n_dp)]
        even = jnp.concatenate(parts[0::2], axis=1)
        odd = jnp.concatenate(parts[1::2], axis=1)
        mine = jnp.where(parity == 0, even, odd)
        return jnp.stack([mine, jnp.where(parity == 0, odd, even)])

    def join_columns(pair):
        even = jnp.where(parity == 0, pair[0], pair[1])
        odd = jnp.where(parity == 0, pair[1], pair[0])
        parts = []
        for i in range(n_dp // 2):
            parts.append(even[:, i * share : (i + 1) * share])
            parts.append(odd[:, i * share : (i + 1) * share])
        return jnp.concatenate(parts, axis=1)

    order = [
        (core * 2 + row) * quarter,
        ((1 - core) * 2 + row) * quarter,
        (core * 2 + 1 - row) * quarter,
        ((1 - core) * 2 + 1 - row) * quarter,
    ]

    def rows_at(x, at):
        return lax.dynamic_slice_in_dim(x, at, quarter, x.ndim - 2)

    def own_order(x):
        return jnp.concatenate([rows_at(x, at) for at in order], axis=0)

    def quarter_of(arrays, which):
        per = 4 // len(arrays)
        return (arrays[which // per], which % per)

    def product(pieces, weights, which, added, dtype, parts=(0, 1)):
        tile = 256 if half % 256 == 0 else half
        out = pl.BlockSpec((len(parts), quarter, tile), lambda i: (0, 0, i))
        terms = []
        for slot, w in enumerate(parts):
            for (left, column, depth), right in zip(pieces, weights):
                array, at = quarter_of(left, which)
                terms.append(
                    (
                        array,
                        pl.BlockSpec(
                            (quarter, depth), lambda i, at=at, column=column: (at, column)
                        ),
                        right[w],
                        pl.BlockSpec((tile, depth), lambda i: (i, 0)),
                        "nt",
                        slot,
                    )
                )

        def finish(sums, extras, outs):
            for slot, total in enumerate(sums):
                for extra in extras:
                    total = total + extra[slot].astype(F32)
                outs[0][slot] = total.astype(dtype)

        return fused_dots(
            (half // tile,),
            terms,
            [(extra, out) for extra in added],
            [((len(parts), quarter, half), dtype, out)],
            finish,
        )[0]

    def reduce_rows(pieces, weights, parts=(0, 1), early={}):

        def one(which, added, dtype):
            lefts, rights = pieces, weights
            if which in early:
                lefts, rights = pieces[-1:], weights[-1:]
                added = [early[which]] + added
            return product(lefts, rights, which, added, dtype, parts)

        far_in = to_core(one(3, [], HALF))
        near_in = to_row(one(2, [far_in], HALF))
        side_in = to_core(one(1, [], HALF))
        return (one(0, [side_in], F32), near_in)

    def spread(x):
        across = to_row(x)
        return [x, to_core(x), across, to_core(across)]

    def gather_outer(piece):
        return lax.all_gather(piece, DP, axis=0, tiled=True, axis_index_groups=outer)

    def gather_model(shard, chunks):
        width = shard.shape[1] // chunks
        found = []
        for j in range(chunks):
            mine = gather_outer(shard[:, j * width : (j + 1) * width])
            found.append((mine, to_twin(mine)))
        return found

    def weight_grad(left, right, which, added):
        right, column, width = right
        tile = 256 if half % 256 == 0 else half
        out = pl.BlockSpec((tile, width), lambda i: (i, 0))
        parts = 1 if len(left) == len(right) == 1 else 4
        rows = tokens // parts
        terms = []
        for p in range(parts):
            piece, at = quarter_of(left, p) if parts > 1 else (left[0], 0)
            other, there = quarter_of(right, p) if parts > 1 else (right[0], 0)
            terms.append(
                (
                    piece,
                    pl.BlockSpec((None, rows, tile), lambda i, at=at: (which, at, i)),
                    other,
                    pl.BlockSpec((rows, width), lambda i, there=there: (there, column)),
                    "tn",
                    0,
                )
            )

        def finish(sums, extras, outs):
            total = sums[0]
            for extra in extras:
                total = total + extra[...].astype(F32)
            outs[0][...] = total.astype(HALF)

        return fused_dots(
            (half // tile,),
            terms,
            [(extra, out) for extra in added],
            [((half, width), HALF, out)],
            finish,
        )[0]

    def scatter_model(left, rights):
        found = []
        for right in rights:
            other = to_twin(weight_grad(left, right, 1, []))
            total = weight_grad(left, right, 0, [other])
            found.append(
                lax.psum_scatter(
                    total, DP, scatter_dimension=0, tiled=True, axis_index_groups=outer
                )
            )
        return jnp.concatenate(found, axis=1) if len(found) > 1 else found[0]

    q_cols = query_weight.shape[1]
    kv_cols = key_projection.shape[1]
    front_width = q_cols + 2 * kv_cols
    gain_block = jnp.concatenate(
        [
            norm_gains.T,
            jnp.pad(head_gains.T, ((0, share - head_gains.shape[1]), (0, 0))),
            jnp.zeros((share, 128 - 6), HALF),
        ],
        axis=1,
    )
    front_shard = jnp.concatenate(
        [query_weight, key_projection, value_projection, gain_block], axis=1
    )
    front = gather_model(front_shard, 1)[0]
    back = gather_model(output_weight.T, 1)[0]
    gates = gather_model(gate_weight, CHUNKS)
    upwards = gather_model(upward_weight, CHUNKS)
    down_shard = down_weight.T
    units = down_weight.shape[0]
    downs = gather_model(down_shard[:, : units // 2], 1)
    for at, tag in ((units // 2, "down1"), (3 * units // 4, "down2")):
        piece = down_shard[:, at : at + units // 4]
        if tag == "down1":
            mine = gather_outer(piece)
            downs.append((mine, to_twin(mine)))
        else:
            twin_piece = to_twin(piece)
            downs.append((gather_outer(piece), gather_outer(twin_piece)))

    gains = jnp.stack([f[:, front_width : front_width + 4].T for f in front]).astype(F32)
    gain = [gains[:, i : i + 1, :] for i in range(4)]
    head_width = head_gains.shape[1]
    head_parts = [
        f[:, front_width + 4 : front_width + 6]
        .reshape(n_dp // 2, share, 2)[:, :head_width, :]
        .astype(F32)
        for f in front
    ]
    head_even = jnp.where(parity == 0, head_parts[0], head_parts[1])
    head_odd = jnp.where(parity == 0, head_parts[1], head_parts[0])
    head_gain = jnp.stack([head_even, head_odd], axis=1).reshape(n_dp * head_width, 2).T

    whole = lambda arrays: (arrays, 0, arrays[0].shape[1])
    rows_pair = split_columns(hidden_in)
    upstream = split_columns(rows_at(cotangent, order[0]))
    rows_pair, upstream = lax.optimization_barrier((rows_pair, upstream))
    rows_f32 = rows_pair.astype(F32)
    factor_all = lax.rsqrt(jnp.mean(rows_f32 * rows_f32, axis=(0, 2), keepdims=True) + NORM_EPS)
    attn_in = (rows_f32 * factor_all * (1.0 + gain[0])).astype(HALF)
    own_in = rows_at(rows_pair, order[0])

    def keep(sums, extras, outs):
        outs[0][...] = sums[0].astype(outs[0].dtype)

    projected = all_rows([attn_in], [front], front_width, [], [F32], keep)[0]
    cosine, sine_table = rope_tables(positions[0], HEAD_WIDTH)
    scale = HEAD_WIDTH ** (-0.5)
    heads = [projected[:, i : i + HEAD_WIDTH] for i in range(0, q_cols + kv_cols, HEAD_WIDTH)]
    queries = q_cols // HEAD_WIDTH
    head_row = lambda i: head_gain[0 if i < queries else 1][None, :]
    head_units, factors, turned = [], [], []
    for i, values in enumerate(heads):
        unit, factor = rms_unit(values)
        head_units.append(unit)
        factors.append(factor)
        turned.append(rotate(unit * (1.0 + head_row(i)), cosine, sine_table).astype(HALF))
    query_scaled = jnp.concatenate([t * HALF(scale) for t in turned[:queries]], axis=1)
    key_heads = jnp.concatenate(turned[queries:], axis=1)
    value_heads = projected[:, q_cols + kv_cols :].astype(HALF)
    lo = first_visible(segment_ids[0])
    attended, lse = attend(query_scaled, key_heads, value_heads, lo)
    attended_own = own_order(attended)
    mine, near = reduce_rows([whole([attended_own])], [back])
    attn_sum, middle, ffn_in = glue(
        [mine, near, own_in], [gain[1], gain[2]], [F32, F32, HALF], 0, glue_one
    )
    ffn_pieces = spread(ffn_in)

    def act(sums, extras, outs):
        value, slope = gelu_parts(sums[0])
        outs[0][...] = (value * sums[1]).astype(HALF)
        outs[1][...] = value.astype(HALF)
        outs[2][...] = (slope * sums[1]).astype(HALF)

    mixed, kept_value, kept_slope = [], [], []
    for j in range(CHUNKS):
        made = all_rows(
            ffn_pieces, [gates[j], upwards[j]], gates[j][0].shape[1], [], [HALF] * 3, act
        )
        mixed.append([made[0]])
        kept_value.append(made[1])
        kept_slope.append(made[2])

    half_units = units // 2
    hidden_parts = [
        (mixed[0], 0, half_units),
        (mixed[1], 1, half_units // 2),
        (mixed[1], 0, half_units // 2),
    ]
    ordered = [downs[0], downs[2], downs[1]]
    mine_a, near_a = reduce_rows(hidden_parts, ordered, (0,))
    early = {q: product(hidden_parts[:-1], ordered[:-1], q, [], F32, (1,)) for q in (3, 2)}
    mine_b, near_b = reduce_rows(hidden_parts, ordered, (1,), early)
    block_pair, ffn_grad, gain_four = glue(
        [mine_a, near_a, mine_b, near_b, middle, upstream], [gain[3]], [HALF, HALF], 1, glue_two
    )

    grad_pieces = spread(ffn_grad)
    down_wgrad = scatter_model(grad_pieces, [hidden_parts[0], hidden_parts[2], hidden_parts[1]])

    def hidden(sums, extras, outs):
        at = 0
        for total in sums:
            part = slice(at, at + total.shape[1])
            outs[0][:, part] = (total * extras[0][:, part].astype(F32)).astype(HALF)
            outs[1][:, part] = (total * extras[1][:, part].astype(F32)).astype(HALF)
            at += total.shape[1]

    gate_back, upward_back = [], []
    for j in range(CHUNKS):
        made = [
            all_rows(
                grad_pieces[2 * p : 2 * p + 2],
                downs[:1] if j == 0 else downs[1:],
                half_units,
                [kept_slope[j], kept_value[j]],
                [HALF] * 2,
                hidden,
                first=2 * p,
            )
            for p in range(2)
        ]
        gate_back.append([m[0] for m in made])
        upward_back.append([m[1] for m in made])

    mine, near = reduce_rows([whole(a) for a in gate_back + upward_back], gates + upwards)
    gate_wgrad = scatter_model(ffn_pieces, [whole(a) for a in gate_back])
    upward_wgrad = scatter_model(ffn_pieces, [whole(a) for a in upward_back])
    middle_grad, attn_grad, gain_three, gain_two = glue(
        [mine, near, middle, upstream, attn_sum], [gain[1], gain[2]], [F32, HALF], 2, glue_three
    )
    attn_pieces = spread(attn_grad)
    spots = jnp.stack(order).astype(jnp.int32) // quarter
    block_output = place_rows(spread(join_columns(block_pair)), spots, HALF)

    grad_natural = all_rows(attn_pieces, [back], q_cols, [], [HALF], keep, order=spots)[0]
    query_grad, key_grad, value_grad = attend_back(
        query_scaled, key_heads, value_heads, grad_natural, lo, lse, attended
    )
    output_wgrad = scatter_model(attn_pieces, [whole([attended_own])])
    flats, sums = [], []
    for i, (unit, factor) in enumerate(zip(head_units, factors)):
        at = i * HEAD_WIDTH if i < queries else (i - queries) * HEAD_WIDTH
        source = query_grad * scale if i < queries else key_grad
        back_turned = rotate(source[:, at : at + HEAD_WIDTH], cosine, -sine_table)
        sums.append(jnp.sum(back_turned * unit, axis=0))
        flats.append(rms_backward(back_turned, unit, factor, head_row(i)).astype(HALF))
    head_part = jnp.stack([sum(sums[:queries]), sum(sums[queries:])])
    front_grad = jnp.concatenate(flats + [value_grad.astype(HALF)], axis=1)
    front_own = own_order(front_grad)
    mine, near = reduce_rows([whole([front_own])], [front])
    front_wgrad = scatter_model([attn_in], [whole([front_grad])])
    input_pair, gain_one = glue([mine, near, own_in, middle_grad], [gain[0]], [HALF], 1, glue_four)
    input_grad = place_rows(spread(join_columns(input_pair)), spots, F32)

    gain_rows = join_columns(jnp.concatenate([gain_one, gain_two, gain_three, gain_four], axis=1))
    flat = jnp.concatenate([gain_rows.reshape(-1), head_part.reshape(-1)]).reshape(-1, 128)
    flat = flat + to_core(flat)
    flat = flat + to_row(flat)
    step_bit = 1
    while step_bit < n_dp:
        swap = [(i, i ^ step_bit) for i in range(n_dp)]
        flat = flat + lax.ppermute(flat, DP, swap)
        step_bit *= 2
    flat = flat.reshape(-1)
    gain_total = flat[: 4 * model].reshape(4, model)
    head_total = flat[4 * model :].reshape(2, -1)
    norms_grad = lax.dynamic_slice_in_dim(gain_total, spot * share, share, 1)
    heads_grad = lax.dynamic_slice_in_dim(head_total, spot * head_width, head_width, 1)

    grad_shards = (
        front_wgrad[:, :q_cols].astype(F32),
        front_wgrad[:, q_cols : q_cols + kv_cols].astype(F32),
        front_wgrad[:, q_cols + kv_cols :].astype(F32),
        output_wgrad.T.astype(F32),
        gate_wgrad.astype(F32),
        upward_wgrad.astype(F32),
        down_wgrad.T.astype(F32),
        norms_grad,
        heads_grad,
    )
    params = (
        query_weight,
        key_projection,
        value_projection,
        output_weight,
        gate_weight,
        upward_weight,
        down_weight,
        norm_gains,
        head_gains,
    )
    means = (
        query_mean,
        key_first_moment,
        value_first_moment,
        output_mean,
        gate_mean,
        upward_mean,
        down_mean,
        norms_mean,
        heads_mean,
    )
    squares = (
        query_square,
        key_second_moment,
        value_second_moment,
        output_square,
        gate_square,
        upward_square,
        down_square,
        norms_square,
        heads_square,
    )
    decays = (DECAY_RATE,) * 7 + (0.0, 0.0)
    results = [
        adam_update(param, grad_item, mean_item, square_item, decay)
        for param, grad_item, mean_item, square_item, decay in zip(
            params, grad_shards, means, squares, decays
        )
    ]
    updated = tuple((item[0] for item in results))
    new_means = tuple((item[1] for item in results))
    new_squares = tuple((item[2] for item in results))
    return (block_output, input_grad) + grad_shards + updated + new_means + new_squares


def shards(n_dp, *arrays):
    return step(n_dp, *arrays)


def solution(mesh):
    in_specs = (
        P(DP, None),
        P(DP, None),
        P(DP, None),
        P(DP, None),
        P(DP, TENSOR),
        P(DP, TENSOR),
        P(DP, TENSOR),
        P(TENSOR, DP),
        P(DP, TENSOR),
        P(DP, TENSOR),
        P(TENSOR, DP),
        P(None, DP),
        P(None, DP),
        P(DP, TENSOR),
        P(DP, TENSOR),
        P(DP, TENSOR),
        P(DP, TENSOR),
        P(DP, TENSOR),
        P(DP, TENSOR),
        P(TENSOR, DP),
        P(TENSOR, DP),
        P(DP, TENSOR),
        P(DP, TENSOR),
        P(DP, TENSOR),
        P(DP, TENSOR),
        P(TENSOR, DP),
        P(TENSOR, DP),
        P(None, DP),
        P(None, DP),
        P(None, DP),
        P(None, DP),
    )
    out_specs = (
        P(DP, None),
        P(DP, None),
        P(DP, TENSOR),
        P(DP, TENSOR),
        P(DP, TENSOR),
        P(TENSOR, DP),
        P(DP, TENSOR),
        P(DP, TENSOR),
        P(TENSOR, DP),
        P(None, DP),
        P(None, DP),
        P(DP, TENSOR),
        P(DP, TENSOR),
        P(DP, TENSOR),
        P(TENSOR, DP),
        P(DP, TENSOR),
        P(DP, TENSOR),
        P(TENSOR, DP),
        P(None, DP),
        P(None, DP),
        P(DP, TENSOR),
        P(DP, TENSOR),
        P(DP, TENSOR),
        P(TENSOR, DP),
        P(DP, TENSOR),
        P(DP, TENSOR),
        P(TENSOR, DP),
        P(None, DP),
        P(None, DP),
        P(DP, TENSOR),
        P(DP, TENSOR),
        P(DP, TENSOR),
        P(TENSOR, DP),
        P(DP, TENSOR),
        P(DP, TENSOR),
        P(TENSOR, DP),
        P(None, DP),
        P(None, DP),
    )
    return jax.shard_map(
        functools.partial(shards, mesh.shape[DP]),
        mesh=mesh,
        in_specs=in_specs,
        out_specs=out_specs,
        check_vma=False,
    )
```

```python
import functools

import jax
import jax.numpy as jnp
from jax import lax
from jax.experimental import pallas as pl
from jax.experimental.pallas import tpu as pltpu
from jax.sharding import PartitionSpec as P

HEAD_WIDTH = 256
WINDOW = 1024
STEP = 4
CHUNKS = 2
BLOCK = 256

NORM_EPS = 1e-06
BETA_ONE = 0.9
BETA_TWO = 0.999
ADAM_EPS = 1e-08
LEARN_RATE = 0.01
DECAY_RATE = 0.1
ROPE_BASE = 10000.0
GELU_COEF = 0.7978845608028654
MASKED = -1e30


DP = "dp"
TENSOR = "tensor"
F32 = jnp.float32
HALF = jnp.bfloat16


def contract(a, b, form):
    dims = ((0 if form[0] == "t" else 1,), (1 if form[1] == "t" else 0,))
    return lax.dot_general(a, b, (dims, ((), ())), preferred_element_type=F32)


def mm(a, b):
    return contract(a, b, "nn")


def mm_nt(a, b):
    return contract(a, b, "nt")


def fused_dots(grid, terms, extras, outs, finish):
    arrays, specs, plan, flops = [], [], [], 0
    steps = 1
    for size in grid:
        steps *= size
    for left, left_spec, right, right_spec, form, slot in terms:
        plan.append((len(arrays), form, slot))
        arrays += [left, right]
        specs += [left_spec, right_spec]
        shape = [n for n in left_spec.block_shape if n is not None]
        other = [n for n in right_spec.block_shape if n is not None]
        columns = other[0] if form[1] == "t" else other[1]
        flops += 2 * steps * shape[0] * shape[1] * columns
    base = len(arrays)
    for extra, spec in extras:
        arrays.append(extra)
        specs.append(spec)
    count = len(arrays)
    slots = 1 + max(slot for _, _, slot in plan)

    def kernel(*refs):
        sums = [None] * slots
        for at, form, slot in plan:
            product = contract(refs[at][...], refs[at + 1][...], form)
            sums[slot] = product if sums[slot] is None else sums[slot] + product
        finish(sums, refs[base:count], refs[count:])

    moved = sum(a.size * a.dtype.itemsize for a in {id(a): a for a in arrays}.values())
    return pl.pallas_call(
        kernel,
        grid=grid,
        in_specs=specs,
        out_specs=[spec for _, _, spec in outs],
        out_shape=[jax.ShapeDtypeStruct(shape, dtype) for shape, dtype, _ in outs],
        compiler_params=pltpu.CompilerParams(
            dimension_semantics=("arbitrary",) * len(grid),
            vmem_limit_bytes=56 * 1024 * 1024,
        ),
        cost_estimate=pl.CostEstimate(flops=flops, bytes_accessed=moved, transcendentals=0),
    )(*arrays)


def rope_tables(places, head_size):
    half_dim = head_size // 2
    frequency = ROPE_BASE ** (-2.0 * jnp.arange(half_dim, dtype=F32) / head_size)
    angles = places.astype(F32)[:, None] * frequency[None, :]
    return (jnp.cos(angles), jnp.sin(angles))


def rotate(values, cosine, sine_table):
    half_dim = values.shape[-1] // 2
    first_half = values[..., :half_dim]
    second_half = values[..., half_dim:]
    return jnp.concatenate(
        [
            first_half * cosine - second_half * sine_table,
            second_half * cosine + first_half * sine_table,
        ],
        axis=-1,
    )


def rms_unit(values):
    factor = lax.rsqrt(jnp.mean(values * values, axis=-1, keepdims=True) + NORM_EPS)
    return (values * factor, factor)


def rms_backward(upstream, normed, factor, gain_row):
    scaled = upstream * (1.0 + gain_row)
    return factor * (scaled - normed * jnp.mean(scaled * normed, axis=-1, keepdims=True))


def gelu_parts(values):
    tangent = jnp.tanh(GELU_COEF * (values + 0.044715 * values * values * values))
    value = 0.5 * values * (1.0 + tangent)
    slope = 0.5 * (1.0 + tangent) + 0.5 * values * (1.0 - tangent * tangent) * GELU_COEF * (
        1.0 + 3.0 * 0.044715 * values * values
    )
    return (value, slope)


def row_sum(values, width):
    total = sum(jnp.sum(v, axis=-1, keepdims=True) for v in values)
    return total / width


def unit_of(values, width):
    factor = lax.rsqrt(row_sum([v * v for v in values], width) + NORM_EPS)
    return ([v * factor for v in values], factor)


def back_of(upstream, units, factor, gains, width):
    scaled = [e * (1.0 + g) for e, g in zip(upstream, gains)]
    mean = row_sum([s * u for s, u in zip(scaled, units)], width)
    return [factor * (s - u * mean) for s, u in zip(scaled, units)]


def halves(ref):
    return [ref[w].astype(F32) for w in range(ref.shape[0])]


def put(ref, pair):
    for w, value in enumerate(pair):
        ref[w] = value.astype(ref.dtype)


def put_sum(ref, upstream, units):
    @pl.when(pl.program_id(0) == 0)
    def _():
        ref[...] = jnp.zeros_like(ref)

    for w, (e, u) in enumerate(zip(upstream, units)):
        ref[w] += jnp.sum(e * u, axis=0, keepdims=True)


def glue(inputs, gains, outs, sums, body):
    rows, half = inputs[0].shape[1:]
    tile = min(64, rows)
    block = lambda n: pl.BlockSpec((n, tile, half), lambda i: (0, i, 0))
    still = pl.BlockSpec((2, 1, half), lambda i: (0, 0, 0))
    return pl.pallas_call(
        body,
        grid=(rows // tile,),
        in_specs=[block(x.shape[0]) for x in inputs] + [still] * len(gains),
        out_specs=[block(2)] * len(outs) + [still] * sums,
        out_shape=[jax.ShapeDtypeStruct((2, rows, half), dtype) for dtype in outs]
        + [jax.ShapeDtypeStruct((2, 1, half), F32)] * sums,
        compiler_params=kernel_params(),
        cost_estimate=pl.CostEstimate(
            flops=64 * rows * half, bytes_accessed=40 * rows * half, transcendentals=0
        ),
    )(*inputs, *gains)


def glue_one(mine, near, own, gain_two, gain_three, sum_ref, middle_ref, ffn_ref):
    width = 2 * mine.shape[2]
    total = [a + b for a, b in zip(halves(mine), halves(near))]
    units, _ = unit_of(total, width)
    middle = [x + u * (1.0 + g) for x, u, g in zip(halves(own), units, halves(gain_two))]
    units, _ = unit_of(middle, width)
    put(sum_ref, total)
    put(middle_ref, middle)
    put(ffn_ref, [u * (1.0 + g) for u, g in zip(units, halves(gain_three))])


def glue_two(
    mine_a, near_a, mine_b, near_b, middle, upstream, gain, block_ref, grad_ref, sum_ref
):
    width = 2 * middle.shape[2]
    total = [mine_a[0] + near_a[0].astype(F32), mine_b[0] + near_b[0].astype(F32)]
    units, factor = unit_of(total, width)
    gains = halves(gain)
    errors = halves(upstream)
    put(block_ref, [x + u * (1.0 + g) for x, u, g in zip(halves(middle), units, gains)])
    put(grad_ref, back_of(errors, units, factor, gains, width))
    put_sum(sum_ref, errors, units)


def glue_three(
    mine, near, middle, upstream, attn_sum, gain_two, gain_three,
    grad_ref, attn_ref, sum_three_ref, sum_two_ref,
):
    width = 2 * middle.shape[2]
    errors = [a + b for a, b in zip(halves(mine), halves(near))]
    units, factor = unit_of(halves(middle), width)
    back = back_of(errors, units, factor, halves(gain_three), width)
    put_sum(sum_three_ref, errors, units)
    grads = [x + y for x, y in zip(halves(upstream), back)]
    put(grad_ref, grads)
    units, factor = unit_of(halves(attn_sum), width)
    put_sum(sum_two_ref, grads, units)
    put(attn_ref, back_of(grads, units, factor, halves(gain_two), width))


def glue_four(mine, near, own, middle_grad, gain_one, out_ref, sum_ref):
    width = 2 * own.shape[2]
    errors = [a + b for a, b in zip(halves(mine), halves(near))]
    units, factor = unit_of(halves(own), width)
    back = back_of(errors, units, factor, halves(gain_one), width)
    put(out_ref, [x + y for x, y in zip(halves(middle_grad), back)])
    put_sum(sum_ref, errors, units)


def take_piece(refs, per, store):
    for k, ref in enumerate(refs):

        @pl.when(pl.program_id(0) // per == k)
        def _(ref=ref):
            store(ref)


def piece_index(per, k):
    return lambda i: jnp.clip(i - k * per, 0, per - 1)


def place_rows(pieces, order, dtype):
    rows, width = pieces[0].shape
    tile = min(128, rows)
    per = rows // tile

    def kernel(order_ref, *refs):
        def store(ref):
            refs[-1][...] = ref[...].astype(dtype)

        take_piece(refs[:-1], per, store)

    specs = [
        pl.BlockSpec((tile, width), lambda i, o, k=k: (piece_index(per, k)(i), 0))
        for k in range(len(pieces))
    ]
    return pl.pallas_call(
        kernel,
        grid_spec=pltpu.PrefetchScalarGridSpec(
            num_scalar_prefetch=1,
            grid=(len(pieces) * per,),
            in_specs=specs,
            out_specs=pl.BlockSpec((tile, width), lambda i, o: (o[i // per] * per + i % per, 0)),
        ),
        out_shape=jax.ShapeDtypeStruct((len(pieces) * rows, width), dtype),
        compiler_params=kernel_params(),
        cost_estimate=pl.CostEstimate(flops=0, bytes_accessed=24 * rows * width, transcendentals=0),
    )(order, *pieces)


def all_rows(pieces, weights, width, extras, outs, finish, first=0, order=None):
    rows, half = pieces[0].shape[1:]
    tile = min(256, rows)
    per = rows // tile
    steps = len(pieces) * per
    count = len(pieces)
    slots = len(weights)

    def kernel(*refs):
        if order is not None:
            refs = refs[1:]
        flat = refs[count : count + 2 * slots]
        rest = refs[count + 2 * slots :]
        if count > 1:
            rest, left = rest[:-1], rest[-1]

            def store(ref):
                left[...] = ref[...]

            take_piece(refs[:count], per, store)
        else:
            left = refs[0]
        sums = [
            contract(left[0], flat[2 * s][...], "nn") + contract(left[1], flat[2 * s + 1][...], "nn")
            for s in range(slots)
        ]
        finish(sums, rest[: len(extras)], rest[len(extras) :])

    specs = [
        pl.BlockSpec((2, tile, half), lambda i, *o, k=k: (0, piece_index(per, k)(i), 0))
        for k in range(count)
    ]
    for pair in weights:
        columns = min(pair[0].shape[1], width)
        specs += [pl.BlockSpec((half, columns), lambda i, *o: (0, 0))] * 2
    skip = first * (rows // tile)
    specs += [pl.BlockSpec((tile, width), lambda i, *o: (skip + i, 0))] * len(extras)
    if order is None:
        target = pl.BlockSpec((tile, width), lambda i: (i, 0))
    else:
        target = pl.BlockSpec((tile, width), lambda i, o: (o[i // per] * per + i % per, 0))
    scratch = [pltpu.VMEM((2, tile, half), HALF)] if count > 1 else []
    arrays = list(pieces) + [w for pair in weights for w in pair] + list(extras)
    return pl.pallas_call(
        kernel,
        grid_spec=pltpu.PrefetchScalarGridSpec(
            num_scalar_prefetch=0 if order is None else 1,
            grid=(steps,),
            in_specs=specs,
            out_specs=[target] * len(outs),
            scratch_shapes=scratch,
        ),
        out_shape=[jax.ShapeDtypeStruct((steps * tile, width), dtype) for dtype in outs],
        compiler_params=pltpu.CompilerParams(
            dimension_semantics=("arbitrary",), vmem_limit_bytes=56 * 1024 * 1024
        ),
        cost_estimate=pl.CostEstimate(
            flops=4 * steps * tile * half * sum(pair[0].shape[1] for pair in weights),
            bytes_accessed=sum(a.size * a.dtype.itemsize for a in arrays),
            transcendentals=0,
        ),
    )(*([] if order is None else [order]), *arrays)


def visible(lo_ref, start, span, heads):
    rows = lax.broadcasted_iota(jnp.int32, (span, BLOCK), 0) + start
    queries = lax.broadcasted_iota(jnp.int32, (1, BLOCK), 1) + pl.program_id(0) * BLOCK
    seen = (rows >= lo_ref[...]) & (rows <= queries)
    return jnp.concatenate([seen] * heads, axis=1)


def stacked(ref, heads):
    width = ref.shape[1] // heads
    return jnp.concatenate([ref[:, h * width : (h + 1) * width] for h in range(heads)], axis=0)


def row_of(ref, heads):
    return jnp.concatenate([ref[h : h + 1, :] for h in range(heads)], axis=1)


def key_start(span):
    end = (pl.program_id(0) + 1) * BLOCK
    return pl.multiple_of(jnp.maximum(end - span, 0), BLOCK)


def attend_kernel(span, heads, q_ref, k_ref, vt_ref, lo_ref, out_ref, lse_ref):
    start = key_start(span)
    width = k_ref.shape[1]
    queries = stacked(q_ref, heads)
    scores = mm_nt(k_ref[pl.ds(start, span), :], queries)
    scores = jnp.where(visible(lo_ref, start, span, heads), scores, MASKED)
    top = jnp.max(scores, axis=0, keepdims=True)
    weights = jnp.exp(scores - top)
    total = jnp.sum(weights, axis=0, keepdims=True)
    result = mm(vt_ref[:, pl.ds(start, span)], weights.astype(HALF)) / total
    lse = top + jnp.log(total)
    for h in range(heads):
        part = slice(h * BLOCK, (h + 1) * BLOCK)
        out_ref[:, h * width : (h + 1) * width] = result[:, part].T.astype(HALF)
        lse_ref[h : h + 1, :] = lse[:, part]


def attend_back_kernel(
    span, heads, q_ref, k_ref, kt_ref, v_ref, do_ref, lo_ref, lse_ref, out_ref,
    dq_ref, dk_ref, dv_ref,
):
    start = key_start(span)
    width = k_ref.shape[1]

    @pl.when(pl.program_id(0) == 0)
    def _():
        dk_ref[...] = jnp.zeros_like(dk_ref)
        dv_ref[...] = jnp.zeros_like(dv_ref)

    keys = pl.ds(start, span)
    queries = stacked(q_ref, heads)
    upstream = stacked(do_ref, heads)
    scores = mm_nt(k_ref[keys, :], queries)
    scores = jnp.where(visible(lo_ref, start, span, heads), scores, MASKED)
    weights = jnp.exp(scores - row_of(lse_ref, heads))
    dv_ref[keys, :] += mm(weights.astype(HALF), upstream)
    weight_grad = mm_nt(v_ref[keys, :], upstream)
    pull = upstream.astype(F32) * stacked(out_ref, heads).astype(F32)
    delta = jnp.sum(pull.T, axis=0, keepdims=True)
    score_grad = (weights * (weight_grad - delta)).astype(HALF)
    dk_ref[keys, :] += mm(score_grad, queries)
    grad = mm(kt_ref[:, keys], score_grad)
    for h in range(heads):
        dq_ref[:, h * width : (h + 1) * width] = grad[:, h * BLOCK : (h + 1) * BLOCK].T


def kernel_params():
    return pltpu.CompilerParams(
        dimension_semantics=("arbitrary",), vmem_limit_bytes=48 * 1024 * 1024
    )


def full_spec(shape):
    return pl.BlockSpec(shape, lambda i: (0,) * len(shape))


def attend(q, k, v, lo):
    length, columns = q.shape
    width = k.shape[1]
    heads = columns // width
    span = min(WINDOW + BLOCK, length)
    rows = pl.BlockSpec((BLOCK, columns), lambda i: (i, 0))
    lane = lambda n: pl.BlockSpec((n, BLOCK), lambda i: (0, i))
    steps = length // BLOCK
    return pl.pallas_call(
        functools.partial(attend_kernel, span, heads),
        grid=(steps,),
        in_specs=[rows, full_spec(k.shape), full_spec((width, length)), lane(1)],
        out_specs=[rows, lane(heads)],
        out_shape=[
            jax.ShapeDtypeStruct(q.shape, HALF),
            jax.ShapeDtypeStruct((heads, length), F32),
        ],
        compiler_params=kernel_params(),
        cost_estimate=pl.CostEstimate(
            flops=4 * steps * span * BLOCK * columns,
            bytes_accessed=4 * length * columns + 4 * length * width,
            transcendentals=steps * span * BLOCK * heads,
        ),
        name="attend",
    )(q, k, v.T, lo)


def attend_back(q, k, v, do, lo, lse, out):
    length, columns = q.shape
    width = k.shape[1]
    heads = columns // width
    span = min(WINDOW + BLOCK, length)
    rows = pl.BlockSpec((BLOCK, columns), lambda i: (i, 0))
    lane = lambda n: pl.BlockSpec((n, BLOCK), lambda i: (0, i))
    steps = length // BLOCK
    return pl.pallas_call(
        functools.partial(attend_back_kernel, span, heads),
        grid=(steps,),
        in_specs=[
            rows, full_spec(k.shape), full_spec((width, length)), full_spec(v.shape), rows,
            lane(1), lane(heads), rows,
        ],
        out_specs=[rows, full_spec(k.shape), full_spec(v.shape)],
        out_shape=[
            jax.ShapeDtypeStruct(q.shape, F32),
            jax.ShapeDtypeStruct(k.shape, F32),
            jax.ShapeDtypeStruct(v.shape, F32),
        ],
        compiler_params=kernel_params(),
        cost_estimate=pl.CostEstimate(
            flops=10 * steps * span * BLOCK * columns,
            bytes_accessed=8 * length * columns + 14 * length * width,
            transcendentals=steps * span * BLOCK * heads,
        ),
        name="attend_back",
    )(q, k, k.T, v, do, lo, lse, out)


def first_visible(segments):
    length = segments.shape[0]
    ids = jnp.arange(length, dtype=jnp.int32)
    begins = jnp.concatenate([jnp.ones((1,), bool), segments[1:] != segments[:-1]])
    starts = lax.cummax(jnp.where(begins, ids, 0), axis=0)
    return jnp.maximum(starts, ids - (WINDOW - 1))[None, :]


def adam_update(weight_shard, grad_shard, mean_shard, square_shard, decay):
    new_mean = BETA_ONE * mean_shard + (1.0 - BETA_ONE) * grad_shard
    new_square = BETA_TWO * square_shard + (1.0 - BETA_TWO) * grad_shard * grad_shard
    mean_hat = new_mean / (1.0 - BETA_ONE**STEP)
    square_hat = new_square / (1.0 - BETA_TWO**STEP)
    weight_value = weight_shard.astype(F32)
    updated = weight_value - LEARN_RATE * (
        mean_hat / (jnp.sqrt(square_hat) + ADAM_EPS) + decay * weight_value
    )
    return (updated, new_mean, new_square)


def step(
    n_dp,
    hidden_in,
    segment_ids,
    positions,
    cotangent,
    query_weight,
    key_projection,
    value_projection,
    output_weight,
    gate_weight,
    upward_weight,
    down_weight,
    norm_gains,
    head_gains,
    query_mean,
    query_square,
    key_first_moment,
    key_second_moment,
    value_first_moment,
    value_second_moment,
    output_mean,
    output_square,
    gate_mean,
    gate_square,
    upward_mean,
    upward_square,
    down_mean,
    down_square,
    norms_mean,
    norms_square,
    heads_mean,
    heads_square,
):
    tokens, model = hidden_in.shape
    share = model // n_dp
    quarter = tokens // 4
    half = model // 2
    spot = lax.axis_index(DP)
    parity = spot % 2
    place = lax.axis_index(TENSOR)
    core = place % 2
    row = place // 2
    outer = [[2 * i + p for i in range(n_dp // 2)] for p in range(2)]
    twins = [(i, i ^ 1) for i in range(n_dp)]

    def to_twin(x):
        return lax.ppermute(x, DP, twins)

    def to_core(x):
        return lax.ppermute(x, TENSOR, [(i, i ^ 1) for i in range(4)])

    def to_row(x):
        return lax.ppermute(x, TENSOR, [(i, i ^ 2) for i in range(4)])

    def split_columns(x):
        parts = [x[:, i * share : (i + 1) * share] for i in range(n_dp)]
        even = jnp.concatenate(parts[0::2], axis=1)
        odd = jnp.concatenate(parts[1::2], axis=1)
        mine = jnp.where(parity == 0, even, odd)
        return jnp.stack([mine, jnp.where(parity == 0, odd, even)])

    def join_columns(pair):
        even = jnp.where(parity == 0, pair[0], pair[1])
        odd = jnp.where(parity == 0, pair[1], pair[0])
        parts = []
        for i in range(n_dp // 2):
            parts.append(even[:, i * share : (i + 1) * share])
            parts.append(odd[:, i * share : (i + 1) * share])
        return jnp.concatenate(parts, axis=1)

    order = [
        (core * 2 + row) * quarter,
        ((1 - core) * 2 + row) * quarter,
        (core * 2 + 1 - row) * quarter,
        ((1 - core) * 2 + 1 - row) * quarter,
    ]

    def rows_at(x, at):
        return lax.dynamic_slice_in_dim(x, at, quarter, x.ndim - 2)

    def own_order(x):
        return jnp.concatenate([rows_at(x, at) for at in order], axis=0)

    def quarter_of(arrays, which):
        per = 4 // len(arrays)
        return (arrays[which // per], which % per)

    def product(pieces, weights, which, added, dtype, parts=(0, 1)):
        tile = 256 if half % 256 == 0 else half
        out = pl.BlockSpec((len(parts), quarter, tile), lambda i: (0, 0, i))
        terms = []
        for slot, w in enumerate(parts):
            for (left, column, depth), right in zip(pieces, weights):
                array, at = quarter_of(left, which)
                terms.append(
                    (
                        array,
                        pl.BlockSpec(
                            (quarter, depth), lambda i, at=at, column=column: (at, column)
                        ),
                        right[w],
                        pl.BlockSpec((tile, depth), lambda i: (i, 0)),
                        "nt",
                        slot,
                    )
                )

        def finish(sums, extras, outs):
            for slot, total in enumerate(sums):
                for extra in extras:
                    total = total + extra[slot].astype(F32)
                outs[0][slot] = total.astype(dtype)

        return fused_dots(
            (half // tile,),
            terms,
            [(extra, out) for extra in added],
            [((len(parts), quarter, half), dtype, out)],
            finish,
        )[0]

    def reduce_rows(pieces, weights, parts=(0, 1), early={}):

        def one(which, added, dtype):
            lefts, rights = pieces, weights
            if which in early:
                lefts, rights = pieces[-1:], weights[-1:]
                added = [early[which]] + added
            return product(lefts, rights, which, added, dtype, parts)

        far_in = to_core(one(3, [], HALF))
        near_in = to_row(one(2, [far_in], HALF))
        side_in = to_core(one(1, [], HALF))
        return (one(0, [side_in], F32), near_in)

    def spread(x):
        across = to_row(x)
        return [x, to_core(x), across, to_core(across)]

    def gather_outer(piece):
        return lax.all_gather(piece, DP, axis=0, tiled=True, axis_index_groups=outer)

    def gather_model(shard, chunks):
        width = shard.shape[1] // chunks
        found = []
        for j in range(chunks):
            mine = gather_outer(shard[:, j * width : (j + 1) * width])
            found.append((mine, to_twin(mine)))
        return found

    def weight_grad(left, right, which, added):
        right, column, width = right
        tile = 256 if half % 256 == 0 else half
        out = pl.BlockSpec((tile, width), lambda i: (i, 0))
        parts = 1 if len(left) == len(right) == 1 else 4
        rows = tokens // parts
        terms = []
        for p in range(parts):
            piece, at = quarter_of(left, p) if parts > 1 else (left[0], 0)
            other, there = quarter_of(right, p) if parts > 1 else (right[0], 0)
            terms.append(
                (
                    piece,
                    pl.BlockSpec((None, rows, tile), lambda i, at=at: (which, at, i)),
                    other,
                    pl.BlockSpec((rows, width), lambda i, there=there: (there, column)),
                    "tn",
                    0,
                )
            )

        def finish(sums, extras, outs):
            total = sums[0]
            for extra in extras:
                total = total + extra[...].astype(F32)
            outs[0][...] = total.astype(HALF)

        return fused_dots(
            (half // tile,),
            terms,
            [(extra, out) for extra in added],
            [((half, width), HALF, out)],
            finish,
        )[0]

    def scatter_outer(total):
        return lax.psum_scatter(total, DP, scatter_dimension=0, tiled=True, axis_index_groups=outer)

    def scatter_model(left, rights, direct=None):
        found = []
        for j, right in enumerate(rights):
            if j == direct:
                far = weight_grad(left, right, 1, [])
                near = weight_grad(left, right, 0, [])
                far = to_twin(scatter_outer(far))
                near = scatter_outer(near)
                found.append((near.astype(F32) + far.astype(F32)).astype(HALF))
                continue
            other = to_twin(weight_grad(left, right, 1, []))
            total = weight_grad(left, right, 0, [other])
            found.append(scatter_outer(total))
        return jnp.concatenate(found, axis=1) if len(found) > 1 else found[0]

    q_cols = query_weight.shape[1]
    kv_cols = key_projection.shape[1]
    front_width = q_cols + 2 * kv_cols
    gain_block = jnp.concatenate(
        [
            norm_gains.T,
            jnp.pad(head_gains.T, ((0, share - head_gains.shape[1]), (0, 0))),
            jnp.zeros((share, 128 - 6), HALF),
        ],
        axis=1,
    )
    front_shard = jnp.concatenate(
        [query_weight, key_projection, value_projection, gain_block], axis=1
    )
    front = gather_model(front_shard, 1)[0]
    back = gather_model(output_weight.T, 1)[0]
    gates = gather_model(gate_weight, CHUNKS)
    upwards = gather_model(upward_weight, CHUNKS)
    down_shard = down_weight.T
    units = down_weight.shape[0]
    downs = gather_model(down_shard[:, : units // 2], 1)
    for at, tag in ((units // 2, "down1"), (3 * units // 4, "down2")):
        piece = down_shard[:, at : at + units // 4]
        if tag == "down1":
            mine = gather_outer(piece)
            downs.append((mine, to_twin(mine)))
        else:
            twin_piece = to_twin(piece)
            downs.append((gather_outer(piece), gather_outer(twin_piece)))

    gains = jnp.stack([f[:, front_width : front_width + 4].T for f in front]).astype(F32)
    gain = [gains[:, i : i + 1, :] for i in range(4)]
    head_width = head_gains.shape[1]
    head_parts = [
        f[:, front_width + 4 : front_width + 6]
        .reshape(n_dp // 2, share, 2)[:, :head_width, :]
        .astype(F32)
        for f in front
    ]
    head_even = jnp.where(parity == 0, head_parts[0], head_parts[1])
    head_odd = jnp.where(parity == 0, head_parts[1], head_parts[0])
    head_gain = jnp.stack([head_even, head_odd], axis=1).reshape(n_dp * head_width, 2).T

    whole = lambda arrays: (arrays, 0, arrays[0].shape[1])
    rows_pair = split_columns(hidden_in)
    upstream = split_columns(rows_at(cotangent, order[0]))
    rows_pair, upstream = lax.optimization_barrier((rows_pair, upstream))
    rows_f32 = rows_pair.astype(F32)
    factor_all = lax.rsqrt(jnp.mean(rows_f32 * rows_f32, axis=(0, 2), keepdims=True) + NORM_EPS)
    attn_in = (rows_f32 * factor_all * (1.0 + gain[0])).astype(HALF)
    own_in = rows_at(rows_pair, order[0])

    def keep(sums, extras, outs):
        outs[0][...] = sums[0].astype(outs[0].dtype)

    projected = all_rows([attn_in], [front], front_width, [], [F32], keep)[0]
    cosine, sine_table = rope_tables(positions[0], HEAD_WIDTH)
    scale = HEAD_WIDTH ** (-0.5)
    heads = [projected[:, i : i + HEAD_WIDTH] for i in range(0, q_cols + kv_cols, HEAD_WIDTH)]
    queries = q_cols // HEAD_WIDTH
    head_row = lambda i: head_gain[0 if i < queries else 1][None, :]
    head_units, factors, turned = [], [], []
    for i, values in enumerate(heads):
        unit, factor = rms_unit(values)
        head_units.append(unit)
        factors.append(factor)
        turned.append(rotate(unit * (1.0 + head_row(i)), cosine, sine_table).astype(HALF))
    query_scaled = jnp.concatenate([t * HALF(scale) for t in turned[:queries]], axis=1)
    key_heads = jnp.concatenate(turned[queries:], axis=1)
    value_heads = projected[:, q_cols + kv_cols :].astype(HALF)
    lo = first_visible(segment_ids[0])
    attended, lse = attend(query_scaled, key_heads, value_heads, lo)
    attended_own = own_order(attended)
    mine, near = reduce_rows([whole([attended_own])], [back])
    attn_sum, middle, ffn_in = glue(
        [mine, near, own_in], [gain[1], gain[2]], [F32, F32, HALF], 0, glue_one
    )
    ffn_pieces = spread(ffn_in)

    def act(sums, extras, outs):
        value, slope = gelu_parts(sums[0])
        outs[0][...] = (value * sums[1]).astype(HALF)
        outs[1][...] = value.astype(HALF)
        outs[2][...] = (slope * sums[1]).astype(HALF)

    mixed, kept_value, kept_slope = [], [], []
    for j in range(CHUNKS):
        made = all_rows(
            ffn_pieces, [gates[j], upwards[j]], gates[j][0].shape[1], [], [HALF] * 3, act
        )
        mixed.append([made[0]])
        kept_value.append(made[1])
        kept_slope.append(made[2])

    half_units = units // 2
    hidden_parts = [
        (mixed[0], 0, half_units),
        (mixed[1], 1, half_units // 2),
        (mixed[1], 0, half_units // 2),
    ]
    ordered = [downs[0], downs[2], downs[1]]
    mine_a, near_a = reduce_rows(hidden_parts, ordered, (0,))
    early = {q: product(hidden_parts[:-1], ordered[:-1], q, [], F32, (1,)) for q in (3, 2)}
    mine_b, near_b = reduce_rows(hidden_parts, ordered, (1,), early)
    block_pair, ffn_grad, gain_four = glue(
        [mine_a, near_a, mine_b, near_b, middle, upstream], [gain[3]], [HALF, HALF], 1, glue_two
    )

    grad_pieces = spread(ffn_grad)
    down_wgrad = scatter_model(
        grad_pieces, [hidden_parts[0], hidden_parts[2], hidden_parts[1]], direct=2
    )

    def hidden(sums, extras, outs):
        at = 0
        for total in sums:
            part = slice(at, at + total.shape[1])
            outs[0][:, part] = (total * extras[0][:, part].astype(F32)).astype(HALF)
            outs[1][:, part] = (total * extras[1][:, part].astype(F32)).astype(HALF)
            at += total.shape[1]

    gate_back, upward_back = [], []
    for j in range(CHUNKS):
        made = [
            all_rows(
                grad_pieces[2 * p : 2 * p + 2],
                downs[:1] if j == 0 else downs[1:],
                half_units,
                [kept_slope[j], kept_value[j]],
                [HALF] * 2,
                hidden,
                first=2 * p,
            )
            for p in range(2)
        ]
        gate_back.append([m[0] for m in made])
        upward_back.append([m[1] for m in made])

    mine, near = reduce_rows([whole(a) for a in gate_back + upward_back], gates + upwards)
    gate_wgrad = scatter_model(ffn_pieces, [whole(a) for a in gate_back])
    upward_wgrad = scatter_model(ffn_pieces, [whole(a) for a in upward_back])
    middle_grad, attn_grad, gain_three, gain_two = glue(
        [mine, near, middle, upstream, attn_sum], [gain[1], gain[2]], [F32, HALF], 2, glue_three
    )
    attn_pieces = spread(attn_grad)
    spots = jnp.stack(order).astype(jnp.int32) // quarter
    block_output = place_rows(spread(join_columns(block_pair)), spots, HALF)

    grad_natural = all_rows(attn_pieces, [back], q_cols, [], [HALF], keep, order=spots)[0]
    query_grad, key_grad, value_grad = attend_back(
        query_scaled, key_heads, value_heads, grad_natural, lo, lse, attended
    )
    output_wgrad = scatter_model(attn_pieces, [whole([attended_own])])
    flats, sums = [], []
    for i, (unit, factor) in enumerate(zip(head_units, factors)):
        at = i * HEAD_WIDTH if i < queries else (i - queries) * HEAD_WIDTH
        source = query_grad * scale if i < queries else key_grad
        back_turned = rotate(source[:, at : at + HEAD_WIDTH], cosine, -sine_table)
        sums.append(jnp.sum(back_turned * unit, axis=0))
        flats.append(rms_backward(back_turned, unit, factor, head_row(i)).astype(HALF))
    head_part = jnp.stack([sum(sums[:queries]), sum(sums[queries:])])
    front_grad = jnp.concatenate(flats + [value_grad.astype(HALF)], axis=1)
    front_own = own_order(front_grad)
    mine, near = reduce_rows([whole([front_own])], [front])
    front_wgrad = scatter_model([attn_in], [whole([front_grad])])
    input_pair, gain_one = glue([mine, near, own_in, middle_grad], [gain[0]], [HALF], 1, glue_four)
    input_grad = place_rows(spread(join_columns(input_pair)), spots, F32)

    gain_rows = join_columns(jnp.concatenate([gain_one, gain_two, gain_three, gain_four], axis=1))
    flat = jnp.concatenate([gain_rows.reshape(-1), head_part.reshape(-1)]).reshape(-1, 128)
    flat = flat + to_core(flat)
    flat = flat + to_row(flat)
    step_bit = 1
    while step_bit < n_dp:
        swap = [(i, i ^ step_bit) for i in range(n_dp)]
        flat = flat + lax.ppermute(flat, DP, swap)
        step_bit *= 2
    flat = flat.reshape(-1)
    gain_total = flat[: 4 * model].reshape(4, model)
    head_total = flat[4 * model :].reshape(2, -1)
    norms_grad = lax.dynamic_slice_in_dim(gain_total, spot * share, share, 1)
    heads_grad = lax.dynamic_slice_in_dim(head_total, spot * head_width, head_width, 1)

    grad_shards = (
        front_wgrad[:, :q_cols].astype(F32),
        front_wgrad[:, q_cols : q_cols + kv_cols].astype(F32),
        front_wgrad[:, q_cols + kv_cols :].astype(F32),
        output_wgrad.T.astype(F32),
        gate_wgrad.astype(F32),
        upward_wgrad.astype(F32),
        down_wgrad.T.astype(F32),
        norms_grad,
        heads_grad,
    )
    params = (
        query_weight,
        key_projection,
        value_projection,
        output_weight,
        gate_weight,
        upward_weight,
        down_weight,
        norm_gains,
        head_gains,
    )
    means = (
        query_mean,
        key_first_moment,
        value_first_moment,
        output_mean,
        gate_mean,
        upward_mean,
        down_mean,
        norms_mean,
        heads_mean,
    )
    squares = (
        query_square,
        key_second_moment,
        value_second_moment,
        output_square,
        gate_square,
        upward_square,
        down_square,
        norms_square,
        heads_square,
    )
    decays = (DECAY_RATE,) * 7 + (0.0, 0.0)
    results = []
    for parts in zip(params, grad_shards, means, squares, decays):
        results.append(adam_update(*parts))
    updated = tuple((item[0] for item in results))
    new_means = tuple((item[1] for item in results))
    new_squares = tuple((item[2] for item in results))
    return (block_output, input_grad) + grad_shards + updated + new_means + new_squares


def shards(n_dp, *arrays):
    return step(n_dp, *arrays)


def solution(mesh):
    in_specs = (
        P(DP, None),
        P(DP, None),
        P(DP, None),
        P(DP, None),
        P(DP, TENSOR),
        P(DP, TENSOR),
        P(DP, TENSOR),
        P(TENSOR, DP),
        P(DP, TENSOR),
        P(DP, TENSOR),
        P(TENSOR, DP),
        P(None, DP),
        P(None, DP),
        P(DP, TENSOR),
        P(DP, TENSOR),
        P(DP, TENSOR),
        P(DP, TENSOR),
        P(DP, TENSOR),
        P(DP, TENSOR),
        P(TENSOR, DP),
        P(TENSOR, DP),
        P(DP, TENSOR),
        P(DP, TENSOR),
        P(DP, TENSOR),
        P(DP, TENSOR),
        P(TENSOR, DP),
        P(TENSOR, DP),
        P(None, DP),
        P(None, DP),
        P(None, DP),
        P(None, DP),
    )
    out_specs = (
        P(DP, None),
        P(DP, None),
        P(DP, TENSOR),
        P(DP, TENSOR),
        P(DP, TENSOR),
        P(TENSOR, DP),
        P(DP, TENSOR),
        P(DP, TENSOR),
        P(TENSOR, DP),
        P(None, DP),
        P(None, DP),
        P(DP, TENSOR),
        P(DP, TENSOR),
        P(DP, TENSOR),
        P(TENSOR, DP),
        P(DP, TENSOR),
        P(DP, TENSOR),
        P(TENSOR, DP),
        P(None, DP),
        P(None, DP),
        P(DP, TENSOR),
        P(DP, TENSOR),
        P(DP, TENSOR),
        P(TENSOR, DP),
        P(DP, TENSOR),
        P(DP, TENSOR),
        P(TENSOR, DP),
        P(None, DP),
        P(None, DP),
        P(DP, TENSOR),
        P(DP, TENSOR),
        P(DP, TENSOR),
        P(TENSOR, DP),
        P(DP, TENSOR),
        P(DP, TENSOR),
        P(TENSOR, DP),
        P(None, DP),
        P(None, DP),
    )
    return jax.shard_map(
        functools.partial(shards, mesh.shape[DP]),
        mesh=mesh,
        in_specs=in_specs,
        out_specs=out_specs,
        check_vma=False,
    )
```
